128 devices in a mesh: req: 32 (over y, z, core), tensor: 4 (over x).
Axes of the slice: x: 4, y: 4, z: 4, core: 2. Of those that a mesh axis runs over, the one named last changes fastest.
Arguments:
- hidden: bfloat16 [32768, 1024], P('req', 'tensor')
- gain: bfloat16 [1024], P('tensor'), may hold values from 0.5 to 1.5
- head: bfloat16 [1024, 32128], P(None, ('req', 'tensor'))
- token_ids: int32 [32768], P('req'), may hold values from 0 to 32127
- lengths: int32 [32], P('req'), may hold values from 1 to 1024, 12288 in all
- prompt_of: int32 [32], P('req'), may hold values from 0 to 3, as said below
Outputs:
- token_logprob: float32 [32768], P(('req', 'tensor'))
- token_entropy: float32 [32768], P(('req', 'tensor'))
- prompt_stats: float32 [4, 2], replicated
The draws below stay inside these ranges and needn't reach their ends.
Inputs may be any that keep to these rules, and one draw needn't show every extreme that they name: The lengths sum to 12288 and the longest is exactly 1024. `prompt_of`: a prompt may have no responses.
All inputs are finite; a program needn't handle non-finite values. No bound on the sum of `lengths` on one device may be relied on, other than what follows from the above.
Results may differ from the reference program's by a relative error of at most 0.0019.
Values may be sent and summed in bfloat16 or wider, within the bound.
A program may use at most 128 MiB of HBM per device.

```python
import math
import jax
import jax.numpy as jnp
import numpy as np
from jax import lax

D = 1024
V = 32128
SLOT = 1024
PROMPTS = 4
RESP = 32
TOKENS = 32768


planted = 8


def plan_layout(key):
    features = jax.random.permutation(jax.random.fold_in(key, 31), D)[:planted]
    signs = jnp.where(jax.random.bernoulli(jax.random.fold_in(key, 32), 0.5, (planted,)), 1.0, -1.0).astype(jnp.float32)
    first_col = jax.random.randint(jax.random.fold_in(key, 33), (), 0, V)
    second_col = (first_col + 1 + jax.random.randint(jax.random.fold_in(key, 34), (), 0, V - 1)) % V
    return (features, signs, first_col, second_col)


def head_matrix(key):
    noise = jnp.clip(jax.random.normal(jax.random.fold_in(key, 11), (D, V), jnp.float32), -6.0, 6.0)
    values = noise * 0.09375
    features, signs, first_col, second_col = plan_layout(key)
    height = 300.0 / math.sqrt(planted * D)
    offset = 2.0 / math.sqrt(planted * D)
    values = values.at[features, first_col].set(height * signs)
    values = values.at[features, second_col].set((height - offset) * signs)
    return values


def draw_head(key, part):
    return head_matrix(key).astype(jnp.bfloat16)


def draw_hidden(key, part):
    noise = jnp.clip(jax.random.normal(jax.random.fold_in(key, 12), (TOKENS, D), jnp.float32), -6.0, 6.0)
    entries = noise
    features, signs, first_col, second_col = plan_layout(key)
    onplan = jnp.zeros((D,), jnp.float32).at[features].set(1.0)
    pattern = jnp.zeros((D,), jnp.float32).at[features].set(signs)
    share = jax.random.uniform(jax.random.fold_in(key, 15), (TOKENS, 1), jnp.float32, 0.7, 0.95)
    strength = jnp.sqrt(share * (D - planted) / (planted * (1.0 - share)))
    aligned = noise * (1.0 - onplan)[None, :] + strength * pattern[None, :]
    drawn = entries * (1.0 - onplan)[None, :]
    chosen = (jnp.arange(TOKENS) % 64 == 0)[:, None]
    values = jnp.where(chosen, aligned, drawn)
    return values.astype(jnp.bfloat16)


def draw_prompt_of(key, part):
    empty = jax.random.randint(jax.random.fold_in(key, 21), (), 1, PROMPTS - 1)
    base = jax.random.randint(jax.random.fold_in(key, 22), (RESP,), 0, PROMPTS - 1)
    values = base + (base >= empty).astype(jnp.int32)
    order = jax.random.permutation(jax.random.fold_in(key, 23), RESP)
    values = values.at[order[0]].set(0)
    values = values.at[order[1]].set(PROMPTS - 1)
    return values.astype(jnp.int32)


def set_ends(array, own_key, low, top_value):
    index_at = [jax.random.randint(jax.random.fold_in(own_key, axis), (), 0, length) for axis, length in enumerate(array.shape)]
    main_axis = array.shape.index(max(array.shape))
    next_to = index_at[:main_axis] + [(index_at[main_axis] + 1) % array.shape[main_axis]] + index_at[main_axis + 1:]
    return array.at[tuple(index_at)].set(low).at[tuple(next_to)].set(top_value)


def length_profile(amount, total, most, lean):
    portions = [(1 << 20) // math.isqrt(rank ** lean) + 1 for rank in range(2, amount + 1)]
    surplus, holding = total - most - (amount - 1), [1] * (amount - 1)
    while surplus > 0:
        candidates = [i for i in range(amount - 1) if holding[i] < most]
        pool, budget = sum([portions[i] for i in candidates]), surplus
        for i in candidates:
            addition = min(most - holding[i], max(1, budget * portions[i] // pool), surplus)
            holding[i] = holding[i] + addition
            surplus = surplus - addition
    return np.array([most] + holding)


def uneven(rng, number_of, total, reach, slope):
    if number_of == 2:
        one = jax.random.randint(rng, (), max(1, total - reach), min(reach, total - 1) + 1)
        return jnp.stack([one, total - one])
    sizes = jnp.asarray(length_profile(number_of, total, reach, slope), jnp.int32)
    couples = (number_of - 1) // 2
    source_of, sink = sizes[1:1 + 2 * couples:2], sizes[2:2 + 2 * couples:2]
    margin = jnp.minimum(source_of - 1, reach - sink)
    moved = jax.random.randint(jax.random.fold_in(rng, 1), (couples,), 0, 1 << 20) % (margin + 1)
    sizes = sizes.at[1:1 + 2 * couples:2].set(source_of - moved).at[2:2 + 2 * couples:2].set(sink + moved)
    return sizes[jax.random.permutation(jax.random.fold_in(rng, 2), number_of)]


def setup_inputs(seed: int = 0) -> dict:
    streams_of = jax.random.split(jax.random.key(seed), 7)
    return {
        "hidden": draw_hidden(jax.random.fold_in(streams_of[6], 71), 0),
        "gain": jnp.clip(1.0 + 0.1 * jax.random.normal(streams_of[1], (D,), jnp.float32), 0.5, 1.5).astype(jnp.bfloat16),
        "head": draw_head(jax.random.fold_in(streams_of[6], 71), 0),
        "token_ids": set_ends(jax.random.randint(streams_of[3], (TOKENS,), 0, V), jax.random.fold_in(streams_of[3], 1), 0, V - 1).astype(jnp.int32),
        "lengths": uneven(streams_of[4], RESP, RESP * SLOT * 3 // 8, SLOT, 2).astype(jnp.int32),
        "prompt_of": draw_prompt_of(jax.random.fold_in(streams_of[6], 71), 0),
    }


eps = 1e-06

def reference(hidden, gain, head, token_ids, lengths, prompt_of):
    widened = hidden.astype(jnp.float32)
    scale = lax.rsqrt(lax.optimization_barrier(jnp.mean(widened * widened, axis=1)) + eps)
    normed = (widened * scale[:, None] * gain.astype(jnp.float32)[None, :]).astype(jnp.bfloat16)
    block = min(512, TOKENS)
    count = TOKENS // block

    def score(pair):
        rows, ids = pair
        logits = jnp.dot(rows, head, preferred_element_type=jnp.float32)
        top = lax.optimization_barrier(jnp.max(logits, axis=1))
        expo = jnp.exp(logits - top[:, None])
        total = lax.optimization_barrier(jnp.sum(expo, axis=1))
        moment = lax.optimization_barrier(jnp.sum(expo * logits, axis=1))
        picked = jnp.take_along_axis(logits, ids[:, None], axis=1)[:, 0]
        log_norm = top + jnp.log(total)
        return (picked - log_norm, log_norm - moment / total)
    logprob, entropy = lax.map(score, (normed.reshape(count, block, D), token_ids.reshape(count, block)))
    logprob = logprob.reshape(TOKENS)
    entropy = entropy.reshape(TOKENS)
    slots = jnp.arange(TOKENS, dtype=jnp.int32)
    owner = slots // SLOT
    live = slots % SLOT < lengths[owner]
    logprob = jnp.where(live, logprob, 0.0)
    entropy = jnp.where(live, entropy, 0.0)
    per_resp = jnp.stack([lax.optimization_barrier(jnp.sum(entropy.reshape(RESP, SLOT), axis=1)), lax.optimization_barrier(jnp.sum(logprob.reshape(RESP, SLOT), axis=1)), lengths.astype(jnp.float32)], axis=1)
    onehot = (prompt_of[:, None] == jnp.arange(PROMPTS, dtype=jnp.int32)[None, :]).astype(jnp.float32)
    totals = lax.optimization_barrier(jnp.sum(onehot[:, :, None] * per_resp[:, None, :], axis=0))
    prompt_stats = totals[:, :2] / jnp.maximum(totals[:, 2:3], 1.0)
    return (logprob, entropy, prompt_stats)
```

```python
import jax
import jax.numpy as jnp
from jax import lax
from jax.sharding import PartitionSpec as P

PROMPTS = 4
NEG = -1e30

eps = 1e-06


def chunk_stats(normed, piece, vocab_ids, valid, ids):
    logits = lax.dot_general(normed, piece, (((1,), (1,)), ((), ())), preferred_element_type=jnp.float32)
    logits = jnp.where(valid[None, :], logits, NEG)
    top = jnp.max(logits, axis=1)
    expo = jnp.exp(logits - top[:, None])
    total = jnp.sum(expo, axis=1)
    moment = jnp.sum(expo * logits, axis=1)
    pick = jnp.sum(jnp.where(vocab_ids[None, :] == ids[:, None], logits, 0.0), axis=1)
    return top, total, moment, pick


def merge(stats):
    tops = jnp.stack([s[0] for s in stats])
    top = jnp.max(tops, axis=0)
    factor = jnp.exp(tops - top[None, :])
    total = jnp.sum(factor * jnp.stack([s[1] for s in stats]), axis=0)
    moment = jnp.sum(factor * jnp.stack([s[2] for s in stats]), axis=0)
    pick = jnp.sum(jnp.stack([s[3] for s in stats]), axis=0)
    return top, total, moment, pick


def local(hidden, gain, head, token_ids, lengths, prompt_of):
    rows, part_width = hidden.shape
    splits = lax.axis_size("tensor")
    column_index = lax.axis_index("tensor")
    req_count = lax.axis_size("req")
    shard_cols = head.shape[1]
    width = part_width * splits

    extra = jnp.zeros((8, part_width), hidden.dtype).at[0].set(gain)
    packed = jnp.concatenate([hidden, extra], axis=0)
    gathered = lax.all_gather(packed, "tensor", axis=1, tiled=True)
    widened = gathered[:rows].astype(jnp.float32)
    gain_full = gathered[rows].astype(jnp.float32)
    scale = lax.rsqrt(jnp.sum(widened * widened, axis=1) / width + eps)
    normed = (widened * scale[:, None] * gain_full[None, :]).astype(jnp.bfloat16)

    head_t = head.T
    chunk = 128
    bounds = [(lo, min(lo + chunk, shard_cols)) for lo in range(0, shard_cols, chunk)]
    stats = []
    for lo, hi in bounds:
        part = head_t[lo:hi]
        if hi - lo < chunk:
            part = jnp.concatenate([part, jnp.zeros((chunk - (hi - lo), part.shape[1]), part.dtype)], axis=0)
        piece = lax.all_gather(part, "req", axis=0, tiled=True)
        g = jnp.arange(req_count * chunk, dtype=jnp.int32)
        owner = g // chunk
        offset = lo + g % chunk
        valid = offset < hi
        vocab_ids = jnp.where(valid, (owner * splits + column_index) * shard_cols + offset, -1)
        stats.append(chunk_stats(normed, piece, vocab_ids, valid, token_ids))
    mine = merge(stats)

    everyone = lax.all_gather(jnp.stack(mine), "tensor", axis=0, tiled=False)
    top, total, moment, picked = merge([tuple(everyone[k, j] for j in range(4)) for k in range(splits)])

    positions = jnp.arange(rows, dtype=jnp.int32)
    live = positions < lengths[0]
    safe_total = jnp.where(live, total, 1.0)
    log_norm = top + jnp.log(safe_total)
    logprob = jnp.where(live, picked - log_norm, 0.0)
    entropy = jnp.where(live, log_norm - moment / safe_total, 0.0)
    onehot = (jnp.arange(PROMPTS, dtype=jnp.int32) == prompt_of[0]).astype(jnp.float32)
    summary = jnp.stack([jnp.sum(entropy), jnp.sum(logprob), lengths[0].astype(jnp.float32)])
    summed = lax.psum(onehot[:, None] * summary[None, :], "req")
    prompt_stats = summed[:, :2] / jnp.maximum(summed[:, 2:3], 1.0)
    share = rows // splits
    own_logprob = lax.dynamic_slice_in_dim(logprob, column_index * share, share)
    own_entropy = lax.dynamic_slice_in_dim(entropy, column_index * share, share)
    return (own_logprob, own_entropy, prompt_stats)


def solution(mesh):
    in_specs = (
        P("req", "tensor"),
        P("tensor"),
        P(None, ("req", "tensor")),
        P("req"),
        P("req"),
        P("req"),
    )
    out_specs = (P(("req", "tensor")), P(("req", "tensor")), P())
    return jax.shard_map(local, mesh=mesh, in_specs=in_specs, out_specs=out_specs, check_vma=False)
```

```python
import jax
import jax.numpy as jnp
from jax import lax
from jax.sharding import PartitionSpec as P
from jax.experimental.layout import Layout, with_layout_constraint

PROMPTS = 4
NEG = -1e30

eps = 1e-06


def chunk_stats(normed, piece, vocab_ids, valid, ids):
    logits = lax.dot_general(normed, piece, (((1,), (1,)), ((), ())), preferred_element_type=jnp.float32)
    logits = jnp.where(valid[None, :], logits, NEG)
    top = jnp.max(logits, axis=1)
    expo = jnp.exp(logits - top[:, None])
    total = jnp.sum(expo, axis=1)
    moment = jnp.sum(expo * logits, axis=1)
    pick = jnp.sum(jnp.where(vocab_ids[None, :] == ids[:, None], logits, 0.0), axis=1)
    return top, total, moment, pick


def merge(stats):
    tops = jnp.stack([s[0] for s in stats])
    top = jnp.max(tops, axis=0)
    factor = jnp.exp(tops - top[None, :])
    total = jnp.sum(factor * jnp.stack([s[1] for s in stats]), axis=0)
    moment = jnp.sum(factor * jnp.stack([s[2] for s in stats]), axis=0)
    pick = jnp.sum(jnp.stack([s[3] for s in stats]), axis=0)
    return top, total, moment, pick


def body(hidden, gain, head, token_ids, lengths, prompt_of):
    rows, part_width = hidden.shape
    splits = lax.axis_size("tensor")
    column_index = lax.axis_index("tensor")
    req_count = lax.axis_size("req")
    shard_cols = head.shape[1]
    width = part_width * splits

    extra = jnp.zeros((8, part_width), hidden.dtype).at[0].set(gain)
    packed = jnp.concatenate([hidden, extra], axis=0)
    stacked = lax.all_gather(packed, "tensor", axis=0, tiled=False)
    gathered = jnp.transpose(stacked, (1, 0, 2)).reshape(rows + 8, width)
    widened = gathered[:rows].astype(jnp.float32)
    gain_full = gathered[rows].astype(jnp.float32)
    scale = lax.rsqrt(jnp.sum(widened * widened, axis=1) / width + eps)
    normed = (widened * scale[:, None] * gain_full[None, :]).astype(jnp.bfloat16)

    chunk = 128
    bounds = [(lo, min(lo + chunk, shard_cols)) for lo in range(0, shard_cols, chunk)]
    stats = []
    for lo, hi in bounds:
        part = head[:, lo:hi].T
        if hi - lo < chunk:
            part = jnp.concatenate([part, jnp.zeros((chunk - (hi - lo), part.shape[1]), part.dtype)], axis=0)
        part = with_layout_constraint(part, Layout(major_to_minor=(0, 1)))
        piece = lax.all_gather(part, "req", axis=0, tiled=False)
        piece = with_layout_constraint(piece, Layout(major_to_minor=(0, 1, 2)))
        piece = piece.reshape(req_count * chunk, piece.shape[2])
        g = jnp.arange(req_count * chunk, dtype=jnp.int32)
        owner = g // chunk
        offset = lo + g % chunk
        valid = offset < hi
        vocab_ids = jnp.where(valid, (owner * splits + column_index) * shard_cols + offset, -1)
        stats.append(chunk_stats(normed, piece, vocab_ids, valid, token_ids))
    mine = merge(stats)

    everyone = lax.all_gather(jnp.stack(mine), "tensor", axis=0, tiled=False)
    top, total, moment, picked = merge([tuple(everyone[k, j] for j in range(4)) for k in range(splits)])

    positions = jnp.arange(rows, dtype=jnp.int32)
    live = positions < lengths[0]
    safe_total = jnp.where(live, total, 1.0)
    log_norm = top + jnp.log(safe_total)
    logprob = jnp.where(live, picked - log_norm, 0.0)
    entropy = jnp.where(live, log_norm - moment / safe_total, 0.0)
    onehot = (jnp.arange(PROMPTS, dtype=jnp.int32) == prompt_of[0]).astype(jnp.float32)
    share = rows // splits
    own_logprob = lax.dynamic_slice_in_dim(logprob, column_index * share, share)
    own_entropy = lax.dynamic_slice_in_dim(entropy, column_index * share, share)
    count = jnp.where(column_index == 0, lengths[0], 0).astype(jnp.float32)
    summary = jnp.stack([jnp.sum(own_entropy), jnp.sum(own_logprob), count])
    summed = lax.psum(onehot[:, None] * summary[None, :], ("req", "tensor"))
    prompt_stats = summed[:, :2] / jnp.maximum(summed[:, 2:3], 1.0)
    return (own_logprob, own_entropy, prompt_stats)


def solution(mesh):
    in_specs = (
        P("req", "tensor"),
        P("tensor"),
        P(None, ("req", "tensor")),
        P("req"),
        P("req"),
        P("req"),
    )
    out_specs = (P(("req", "tensor")), P(("req", "tensor")), P())
    return jax.shard_map(body, mesh=mesh, in_specs=in_specs, out_specs=out_specs, check_vma=False)
```

```python
import jax
import jax.numpy as jnp
from jax import lax
from jax.sharding import Mesh, PartitionSpec as P
from jax.experimental.layout import Layout, with_layout_constraint

PROMPTS = 4
REQ = ("y", "z", "c")
NEG = -1e30

eps = 1e-06


def chunk_stats(normed, piece, vocab_ids, valid, ids):
    logits = lax.dot_general(normed, piece, (((1,), (1,)), ((), ())), preferred_element_type=jnp.float32)
    logits = jnp.where(valid[None, :], logits, NEG)
    top = jnp.max(logits, axis=1)
    expo = jnp.exp(logits - top[:, None])
    total = jnp.sum(expo, axis=1)
    moment = jnp.sum(expo * logits, axis=1)
    pick = jnp.sum(jnp.where(vocab_ids[None, :] == ids[:, None], logits, 0.0), axis=1)
    return top, total, moment, pick


def merge(stats):
    tops = jnp.stack([s[0] for s in stats])
    top = jnp.max(tops, axis=0)
    factor = jnp.exp(tops - top[None, :])
    total = jnp.sum(factor * jnp.stack([s[1] for s in stats]), axis=0)
    moment = jnp.sum(factor * jnp.stack([s[2] for s in stats]), axis=0)
    pick = jnp.sum(jnp.stack([s[3] for s in stats]), axis=0)
    return top, total, moment, pick


def body(hidden, gain, head, token_ids, lengths, prompt_of):
    rows, part_width = hidden.shape
    splits = lax.axis_size("x")
    column_index = lax.axis_index("x")
    req_count = lax.axis_size(REQ)
    shard_cols = head.shape[1]
    width = part_width * splits

    extra = jnp.zeros((8, part_width), hidden.dtype).at[0].set(gain)
    packed = jnp.concatenate([hidden, extra], axis=0)
    shift = lambda x, d: lax.ppermute(x, "x", [(i, (i + d) % splits) for i in range(splits)])
    from_left = shift(packed, 1)
    from_right = shift(packed, -1)
    from_far = shift(from_left, 1)
    stacked = jnp.stack([packed, from_right, from_far, from_left])
    order = (jnp.arange(splits, dtype=jnp.int32) - column_index) % splits
    stacked = jnp.take(stacked, order, axis=0)
    gathered = jnp.transpose(stacked, (1, 0, 2)).reshape(rows + 8, width)
    widened = gathered[:rows].astype(jnp.float32)
    gain_full = gathered[rows].astype(jnp.float32)
    scale = lax.rsqrt(jnp.sum(widened * widened, axis=1) / width + eps)
    normed = (widened * scale[:, None] * gain_full[None, :]).astype(jnp.bfloat16)

    chunk = 128
    bounds = [(lo, min(lo + chunk, shard_cols)) for lo in range(0, shard_cols, chunk)]
    stats = []
    for lo, hi in bounds:
        part = head[:, lo:hi].T
        if hi - lo < chunk:
            part = jnp.concatenate([part, jnp.zeros((chunk - (hi - lo), part.shape[1]), part.dtype)], axis=0)
        part = with_layout_constraint(part, Layout(major_to_minor=(0, 1)))
        piece = lax.all_gather(part, REQ, axis=0, tiled=False)
        piece = with_layout_constraint(piece, Layout(major_to_minor=(0, 1, 2)))
        piece = piece.reshape(req_count * chunk, piece.shape[2])
        g = jnp.arange(req_count * chunk, dtype=jnp.int32)
        owner = g // chunk
        offset = lo + g % chunk
        valid = offset < hi
        vocab_ids = jnp.where(valid, (owner * splits + column_index) * shard_cols + offset, -1)
        stats.append(chunk_stats(normed, piece, vocab_ids, valid, token_ids))
    mine = merge(stats)

    everyone = lax.all_gather(jnp.stack(mine), "x", axis=0, tiled=False)
    top, total, moment, picked = merge([tuple(everyone[k, j] for j in range(4)) for k in range(splits)])

    positions = jnp.arange(rows, dtype=jnp.int32)
    live = positions < lengths[0]
    safe_total = jnp.where(live, total, 1.0)
    log_norm = top + jnp.log(safe_total)
    logprob = jnp.where(live, picked - log_norm, 0.0)
    entropy = jnp.where(live, log_norm - moment / safe_total, 0.0)
    onehot = (jnp.arange(PROMPTS, dtype=jnp.int32) == prompt_of[0]).astype(jnp.float32)
    share = rows // splits
    own_logprob = lax.dynamic_slice_in_dim(logprob, column_index * share, share)
    own_entropy = lax.dynamic_slice_in_dim(entropy, column_index * share, share)
    count = jnp.where(column_index == 0, lengths[0], 0).astype(jnp.float32)
    summary = jnp.stack([jnp.sum(own_entropy), jnp.sum(own_logprob), count])
    summed = onehot[:, None] * summary[None, :]
    for name in ("c", "z", "y", "x"):
        summed = lax.psum(summed, name)
    prompt_stats = summed[:, :2] / jnp.maximum(summed[:, 2:3], 1.0)
    return (own_logprob, own_entropy, prompt_stats)


def solution(mesh):
    req_axes = mesh.devices.shape[0] // 8
    fine = Mesh(mesh.devices.reshape(req_axes, 4, 2, mesh.devices.shape[1]), ("y", "z", "c", "x"))
    in_specs = (
        P(REQ, "x"),
        P("x"),
        P(None, REQ + ("x",)),
        P(REQ),
        P(REQ),
        P(REQ),
    )
    out_specs = (P(REQ + ("x",)), P(REQ + ("x",)), P())
    return jax.shard_map(body, mesh=fine, in_specs=in_specs, out_specs=out_specs, check_vma=False)
```

```python
import jax
import jax.numpy as jnp
from jax import lax
from jax.sharding import Mesh, PartitionSpec as P
from jax.experimental.layout import Layout, with_layout_constraint

PROMPTS = 4
REQ = ("y", "z", "c")
NEG = -1e30

eps = 1e-06


def chunk_stats(normed, piece, vocab_ids, valid, ids):
    logits = lax.dot_general(normed, piece, (((1,), (1,)), ((), ())), preferred_element_type=jnp.float32)
    logits = jnp.where(valid[None, :], logits, NEG)
    top = jnp.max(logits, axis=1)
    expo = jnp.exp(logits - top[:, None])
    total = jnp.sum(expo, axis=1)
    moment = jnp.sum(expo * logits, axis=1)
    pick = jnp.sum(jnp.where(vocab_ids[None, :] == ids[:, None], logits, 0.0), axis=1)
    return top, total, moment, pick


def merge(stats):
    tops = jnp.stack([s[0] for s in stats])
    top = jnp.max(tops, axis=0)
    factor = jnp.exp(tops - top[None, :])
    total = jnp.sum(factor * jnp.stack([s[1] for s in stats]), axis=0)
    moment = jnp.sum(factor * jnp.stack([s[2] for s in stats]), axis=0)
    pick = jnp.sum(jnp.stack([s[3] for s in stats]), axis=0)
    return top, total, moment, pick


def body(hidden, gain, head, token_ids, lengths, prompt_of):
    rows, part_width = hidden.shape
    splits = lax.axis_size("x")
    column_index = lax.axis_index("x")
    req_count = lax.axis_size(REQ)
    shard_cols = head.shape[1]
    width = part_width * splits

    extra = jnp.zeros((8, part_width), hidden.dtype).at[0].set(gain)
    packed = jnp.concatenate([hidden, extra], axis=0)
    shift = lambda x, d: lax.ppermute(x, "x", [(i, (i + d) % splits) for i in range(splits)])
    from_left = shift(packed, 1)
    from_right = shift(packed, -1)
    from_far = shift(from_left, 1)
    stacked = jnp.stack([packed, from_right, from_far, from_left])
    order = (jnp.arange(splits, dtype=jnp.int32) - column_index) % splits
    stacked = jnp.take(stacked, order, axis=0)
    gathered = jnp.transpose(stacked, (1, 0, 2)).reshape(rows + 8, width)
    widened = gathered[:rows].astype(jnp.float32)
    gain_full = gathered[rows].astype(jnp.float32)
    scale = lax.rsqrt(jnp.sum(widened * widened, axis=1) / width + eps)
    normed = (widened * scale[:, None] * gain_full[None, :]).astype(jnp.bfloat16)

    chunk = 256
    bounds = [(lo, min(lo + chunk, shard_cols)) for lo in range(0, shard_cols, chunk)]
    stats = []
    for lo, hi in bounds:
        part = head[:, lo:hi].T
        if hi - lo < chunk:
            part = jnp.concatenate([part, jnp.zeros((chunk - (hi - lo), part.shape[1]), part.dtype)], axis=0)
        part = with_layout_constraint(part, Layout(major_to_minor=(0, 1)))
        piece = lax.all_gather(part, REQ, axis=0, tiled=False)
        piece = with_layout_constraint(piece, Layout(major_to_minor=(0, 1, 2)))
        piece = piece.reshape(req_count * chunk, piece.shape[2])
        g = jnp.arange(req_count * chunk, dtype=jnp.int32)
        owner = g // chunk
        offset = lo + g % chunk
        valid = offset < hi
        vocab_ids = jnp.where(valid, (owner * splits + column_index) * shard_cols + offset, -1)
        stats.append(chunk_stats(normed, piece, vocab_ids, valid, token_ids))
    mine = merge(stats)

    everyone = lax.all_gather(jnp.stack(mine), "x", axis=0, tiled=False)
    top, total, moment, picked = merge([tuple(everyone[k, j] for j in range(4)) for k in range(splits)])

    positions = jnp.arange(rows, dtype=jnp.int32)
    live = positions < lengths[0]
    safe_total = jnp.where(live, total, 1.0)
    log_norm = top + jnp.log(safe_total)
    logprob = jnp.where(live, picked - log_norm, 0.0)
    entropy = jnp.where(live, log_norm - moment / safe_total, 0.0)
    onehot = (jnp.arange(PROMPTS, dtype=jnp.int32) == prompt_of[0]).astype(jnp.float32)
    share = rows // splits
    own_logprob = lax.dynamic_slice_in_dim(logprob, column_index * share, share)
    own_entropy = lax.dynamic_slice_in_dim(entropy, column_index * share, share)
    summary = jnp.stack([jnp.sum(entropy), jnp.sum(logprob), lengths[0].astype(jnp.float32)])
    summed = onehot[:, None] * summary[None, :]
    for name in REQ[::-1]:
        summed = lax.psum(summed, name)
    prompt_stats = summed[:, :2] / jnp.maximum(summed[:, 2:3], 1.0)
    return (own_logprob, own_entropy, prompt_stats)


def solution(mesh):
    req_axes = mesh.devices.shape[0] // 8
    fine = Mesh(mesh.devices.reshape(req_axes, 4, 2, mesh.devices.shape[1]), ("y", "z", "c", "x"))
    in_specs = (
        P(REQ, "x"),
        P("x"),
        P(None, REQ + ("x",)),
        P(REQ),
        P(REQ),
        P(REQ),
    )
    out_specs = (P(REQ + ("x",)), P(REQ + ("x",)), P())
    return jax.shard_map(body, mesh=fine, in_specs=in_specs, out_specs=out_specs, check_vma=False)
```

```python
import jax
import jax.numpy as jnp
from jax import lax
from jax.sharding import Mesh, PartitionSpec as P
from jax.experimental.layout import Layout, with_layout_constraint

PROMPTS = 4
REQ = ("y", "z", "c")
NEG = -1e30

eps = 1e-06


def chunk_stats(normed, piece, vocab_ids, valid, ids):
    logits = lax.dot_general(normed, piece, (((1,), (1,)), ((), ())), preferred_element_type=jnp.float32)
    logits = jnp.where(valid[None, :], logits, NEG)
    top = jnp.max(logits, axis=1)
    expo = jnp.exp(logits - top[:, None])
    total = jnp.sum(expo, axis=1)
    moment = jnp.sum(expo * logits, axis=1)
    pick = jnp.sum(jnp.where(vocab_ids[None, :] == ids[:, None], logits, 0.0), axis=1)
    return top, total, moment, pick


def merge(stats):
    tops = jnp.stack([s[0] for s in stats])
    top = jnp.max(tops, axis=0)
    factor = jnp.exp(tops - top[None, :])
    total = jnp.sum(factor * jnp.stack([s[1] for s in stats]), axis=0)
    moment = jnp.sum(factor * jnp.stack([s[2] for s in stats]), axis=0)
    pick = jnp.sum(jnp.stack([s[3] for s in stats]), axis=0)
    return top, total, moment, pick


def body(hidden, gain, head, token_ids, lengths, prompt_of):
    rows, part_width = hidden.shape
    splits = lax.axis_size("x")
    column_index = lax.axis_index("x")
    shard_cols = head.shape[1]
    width = part_width * splits

    extra = jnp.zeros((8, part_width), hidden.dtype).at[0].set(gain)
    packed = jnp.concatenate([hidden, extra], axis=0)
    shift = lambda x, d: lax.ppermute(x, "x", [(i, (i + d) % splits) for i in range(splits)])
    from_left = shift(packed, 1)
    from_right = shift(packed, -1)
    from_far = shift(from_left, 1)
    stacked = jnp.stack([packed, from_right, from_far, from_left])
    order = (jnp.arange(splits, dtype=jnp.int32) - column_index) % splits
    stacked = jnp.take(stacked, order, axis=0)
    gathered = jnp.transpose(stacked, (1, 0, 2)).reshape(rows + 8, width)
    widened = gathered[:rows].astype(jnp.float32)
    gain_full = gathered[rows].astype(jnp.float32)
    scale = lax.rsqrt(jnp.sum(widened * widened, axis=1) / width + eps)
    normed = (widened * scale[:, None] * gain_full[None, :]).astype(jnp.bfloat16)

    chunk = 256
    part = head.T
    part = jnp.concatenate([part, jnp.zeros((chunk - shard_cols, part.shape[1]), part.dtype)], axis=0)
    part = with_layout_constraint(part, Layout(major_to_minor=(0, 1)))
    plane = lax.all_gather(part, ("y", "z"), axis=0, tiled=False)
    plane = with_layout_constraint(plane, Layout(major_to_minor=(0, 1, 2)))
    core = lax.axis_index("c")
    cores = lax.axis_size("c")
    blocks = plane.shape[0]
    g = jnp.arange(blocks * chunk, dtype=jnp.int32)
    offset = g % chunk
    valid = offset < shard_cols

    def ids_for(c):
        owner = (g // chunk) * cores + c
        return jnp.where(valid, (owner * splits + column_index) * shard_cols + offset, -1)

    other = lax.ppermute(plane, "c", [(i, (i + 1) % cores) for i in range(cores)])
    first = chunk_stats(normed, plane.reshape(blocks * chunk, -1), ids_for(core), valid, token_ids)
    first, normed_later = lax.optimization_barrier((first, normed))
    second = chunk_stats(normed_later, other.reshape(blocks * chunk, -1), ids_for((core + 1) % cores), valid, token_ids)
    stats = [first, second]
    mine = merge(stats)

    everyone = lax.all_gather(jnp.stack(mine), "x", axis=0, tiled=False)
    top, total, moment, picked = merge([tuple(everyone[k, j] for j in range(4)) for k in range(splits)])

    positions = jnp.arange(rows, dtype=jnp.int32)
    live = positions < lengths[0]
    safe_total = jnp.where(live, total, 1.0)
    log_norm = top + jnp.log(safe_total)
    logprob = jnp.where(live, picked - log_norm, 0.0)
    entropy = jnp.where(live, log_norm - moment / safe_total, 0.0)
    onehot = (jnp.arange(PROMPTS, dtype=jnp.int32) == prompt_of[0]).astype(jnp.float32)
    share = rows // splits
    own_logprob = lax.dynamic_slice_in_dim(logprob, column_index * share, share)
    own_entropy = lax.dynamic_slice_in_dim(entropy, column_index * share, share)
    summary = jnp.stack([jnp.sum(entropy), jnp.sum(logprob), lengths[0].astype(jnp.float32)])
    summed = onehot[:, None] * summary[None, :]
    for name in REQ[::-1]:
        summed = lax.psum(summed, name)
    prompt_stats = summed[:, :2] / jnp.maximum(summed[:, 2:3], 1.0)
    return (own_logprob, own_entropy, prompt_stats)


def solution(mesh):
    req_axes = mesh.devices.shape[0] // 8
    fine = Mesh(mesh.devices.reshape(req_axes, 4, 2, mesh.devices.shape[1]), ("y", "z", "c", "x"))
    in_specs = (
        P(REQ, "x"),
        P("x"),
        P(None, REQ + ("x",)),
        P(REQ),
        P(REQ),
        P(REQ),
    )
    out_specs = (P(REQ + ("x",)), P(REQ + ("x",)), P())
    return jax.shard_map(body, mesh=fine, in_specs=in_specs, out_specs=out_specs, check_vma=False)
```

```python
import functools

import jax
import jax.numpy as jnp
from jax import lax
from jax.experimental import pallas as pl
from jax.experimental.pallas import tpu as pltpu
from jax.sharding import Mesh, PartitionSpec as P
from jax.experimental.layout import Layout, with_layout_constraint

PROMPTS = 4
REQ = ("y", "z", "c")
NEG = -1e30

eps = 1e-06


def stats_kernel(steps, x_ref, w_ref, b_ref, top_ref, tot_ref, mom_ref, m_sc, s_sc, mo_sc):
    j = pl.program_id(1)

    @pl.when(j == 0)
    def _():
        m_sc[...] = jnp.full(m_sc.shape, NEG, jnp.float32)
        s_sc[...] = jnp.zeros(s_sc.shape, jnp.float32)
        mo_sc[...] = jnp.zeros(mo_sc.shape, jnp.float32)

    logits = lax.dot_general(x_ref[...], w_ref[...], (((1,), (1,)), ((), ())), preferred_element_type=jnp.float32)
    logits = logits + b_ref[...]
    m_old = m_sc[...]
    m_new = jnp.maximum(m_old, jnp.max(logits, axis=1, keepdims=True))
    e = jnp.exp(logits - m_new)
    alpha = jnp.exp(m_old - m_new)
    s_sc[...] = s_sc[...] * alpha + jnp.sum(e, axis=1, keepdims=True)
    mo_sc[...] = mo_sc[...] * alpha + jnp.sum(e * logits, axis=1, keepdims=True)
    m_sc[...] = m_new

    @pl.when(j == steps - 1)
    def _():
        top_ref[...] = m_sc[...]
        tot_ref[...] = s_sc[...]
        mom_ref[...] = mo_sc[...]


def fused_stats(normed, piece, bias, tm=512, tn=512):
    rows, depth = normed.shape
    cols = piece.shape[0]
    grid = (rows // tm, cols // tn)
    stat = jax.ShapeDtypeStruct((rows, 1), jnp.float32)
    stat_spec = pl.BlockSpec((tm, 1), lambda i, j: (i, 0))
    return pl.pallas_call(
        functools.partial(stats_kernel, grid[1]),
        out_shape=(stat, stat, stat),
        grid=grid,
        in_specs=[
            pl.BlockSpec((tm, depth), lambda i, j: (i, 0)),
            pl.BlockSpec((tn, depth), lambda i, j: (j, 0)),
            pl.BlockSpec((1, tn), lambda i, j: (0, j)),
        ],
        out_specs=(stat_spec, stat_spec, stat_spec),
        scratch_shapes=[pltpu.VMEM((tm, 1), jnp.float32)] * 3,
        compiler_params=pltpu.CompilerParams(dimension_semantics=("arbitrary", "arbitrary")),
        cost_estimate=pl.CostEstimate(
            flops=2 * rows * cols * depth,
            transcendentals=rows * cols,
            bytes_accessed=2 * (rows * depth + grid[0] * cols * depth),
        ),
    )(normed, piece, bias)


def chunk_stats(normed, piece, valid, position, found):
    bias = jnp.where(valid, 0.0, NEG).astype(jnp.float32)[None, :]
    top, total, moment = fused_stats(normed, piece, bias)
    rows_of = jnp.take(piece, position, axis=0).astype(jnp.float32)
    pick = jnp.where(found, jnp.sum(rows_of * normed.astype(jnp.float32), axis=1), 0.0)
    return top[:, 0], total[:, 0], moment[:, 0], pick


def merge(stats):
    tops = jnp.stack([s[0] for s in stats])
    top = jnp.max(tops, axis=0)
    factor = jnp.exp(tops - top[None, :])
    total = jnp.sum(factor * jnp.stack([s[1] for s in stats]), axis=0)
    moment = jnp.sum(factor * jnp.stack([s[2] for s in stats]), axis=0)
    pick = jnp.sum(jnp.stack([s[3] for s in stats]), axis=0)
    return top, total, moment, pick


def body(hidden, gain, head, token_ids, lengths, prompt_of):
    rows, part_width = hidden.shape
    splits = lax.axis_size("x")
    column_index = lax.axis_index("x")
    req_count = lax.axis_size(REQ)
    shard_cols = head.shape[1]
    width = part_width * splits

    extra = jnp.zeros((8, part_width), hidden.dtype).at[0].set(gain)
    packed = jnp.concatenate([hidden, extra], axis=0)
    shift = lambda x, d: lax.ppermute(x, "x", [(i, (i + d) % splits) for i in range(splits)])
    from_left = shift(packed, 1)
    from_right = shift(packed, -1)
    from_far = shift(from_left, 1)
    stacked = jnp.stack([packed, from_right, from_far, from_left])
    order = (jnp.arange(splits, dtype=jnp.int32) - column_index) % splits
    stacked = jnp.take(stacked, order, axis=0)
    gathered = jnp.transpose(stacked, (1, 0, 2)).reshape(rows + 8, width)
    widened = gathered[:rows].astype(jnp.float32)
    gain_full = gathered[rows].astype(jnp.float32)
    scale = lax.rsqrt(jnp.sum(widened * widened, axis=1) / width + eps)
    normed = (widened * scale[:, None] * gain_full[None, :]).astype(jnp.bfloat16)

    chunk = 256
    bounds = [(lo, min(lo + chunk, shard_cols)) for lo in range(0, shard_cols, chunk)]
    stats = []
    for lo, hi in bounds:
        part = head[:, lo:hi].T
        if hi - lo < chunk:
            part = jnp.concatenate([part, jnp.zeros((chunk - (hi - lo), part.shape[1]), part.dtype)], axis=0)
        part = with_layout_constraint(part, Layout(major_to_minor=(0, 1)))
        piece = lax.all_gather(part, REQ, axis=0, tiled=False)
        piece = with_layout_constraint(piece, Layout(major_to_minor=(0, 1, 2)))
        piece = piece.reshape(req_count * chunk, piece.shape[2])
        g = jnp.arange(req_count * chunk, dtype=jnp.int32)
        owner = g // chunk
        offset = lo + g % chunk
        valid = offset < hi
        vocab_ids = jnp.where(valid, (owner * splits + column_index) * shard_cols + offset, -1)
        block = token_ids // shard_cols
        found = block % splits == column_index
        position = (block // splits) * chunk + token_ids % shard_cols - lo
        stats.append(chunk_stats(normed, piece, valid, position, found))
    mine = merge(stats)

    everyone = lax.all_gather(jnp.stack(mine), "x", axis=0, tiled=False)
    top, total, moment, picked = merge([tuple(everyone[k, j] for j in range(4)) for k in range(splits)])

    positions = jnp.arange(rows, dtype=jnp.int32)
    live = positions < lengths[0]
    safe_total = jnp.where(live, total, 1.0)
    log_norm = top + jnp.log(safe_total)
    logprob = jnp.where(live, picked - log_norm, 0.0)
    entropy = jnp.where(live, log_norm - moment / safe_total, 0.0)
    onehot = (jnp.arange(PROMPTS, dtype=jnp.int32) == prompt_of[0]).astype(jnp.float32)
    share = rows // splits
    own_logprob = lax.dynamic_slice_in_dim(logprob, column_index * share, share)
    own_entropy = lax.dynamic_slice_in_dim(entropy, column_index * share, share)
    summary = jnp.stack([jnp.sum(entropy), jnp.sum(logprob), lengths[0].astype(jnp.float32)])
    summed = onehot[:, None] * summary[None, :]
    for name in REQ[::-1]:
        summed = lax.psum(summed, name)
    prompt_stats = summed[:, :2] / jnp.maximum(summed[:, 2:3], 1.0)
    return (own_logprob, own_entropy, prompt_stats)


def solution(mesh):
    req_axes = mesh.devices.shape[0] // 8
    fine = Mesh(mesh.devices.reshape(req_axes, 4, 2, mesh.devices.shape[1]), ("y", "z", "c", "x"))
    in_specs = (
        P(REQ, "x"),
        P("x"),
        P(None, REQ + ("x",)),
        P(REQ),
        P(REQ),
        P(REQ),
    )
    out_specs = (P(REQ + ("x",)), P(REQ + ("x",)), P())
    return jax.shard_map(body, mesh=fine, in_specs=in_specs, out_specs=out_specs, check_vma=False)
```

```python
import functools

import jax
import jax.numpy as jnp
from jax import lax
from jax.experimental import pallas as pl
from jax.experimental.pallas import tpu as pltpu
from jax.sharding import Mesh, PartitionSpec as P
from jax.experimental.layout import Layout, with_layout_constraint

PROMPTS = 4
REQ = ("y", "z", "c")
NEG = -1e30
LANES = 128

eps = 1e-06


def stats_kernel(steps, x_ref, w_ref, b_ref, v_ref, t_ref, top_ref, tot_ref, mom_ref, pick_ref, m_sc, s_sc, mo_sc, p_sc):
    j = pl.program_id(1)

    @pl.when(j == 0)
    def _():
        m_sc[...] = jnp.full(m_sc.shape, NEG, jnp.float32)
        s_sc[...] = jnp.zeros(s_sc.shape, jnp.float32)
        mo_sc[...] = jnp.zeros(mo_sc.shape, jnp.float32)
        p_sc[...] = jnp.zeros(p_sc.shape, jnp.float32)

    logits = lax.dot_general(x_ref[...], w_ref[...], (((1,), (1,)), ((), ())), preferred_element_type=jnp.float32)
    logits = logits + b_ref[...]
    slabs = logits.shape[1] // LANES
    lane_max = logits[:, :LANES]
    for k in range(1, slabs):
        lane_max = jnp.maximum(lane_max, logits[:, k * LANES:(k + 1) * LANES])
    m_old = m_sc[...]
    m_new = jnp.maximum(m_old, jnp.max(lane_max, axis=1, keepdims=True))
    alpha = jnp.exp(m_old - m_new)
    s = s_sc[...] * alpha
    mo = mo_sc[...] * alpha
    p = p_sc[...]
    tok = t_ref[...]
    for k in range(slabs):
        l = logits[:, k * LANES:(k + 1) * LANES]
        e = jnp.exp(l - m_new)
        s = s + e
        mo = mo + e * l
        p = p + jnp.where(v_ref[:, k * LANES:(k + 1) * LANES] == tok, l, 0.0)
    s_sc[...] = s
    mo_sc[...] = mo
    p_sc[...] = p
    m_sc[...] = m_new

    @pl.when(j == steps - 1)
    def _():
        top_ref[...] = m_sc[...]
        tot_ref[...] = jnp.sum(s_sc[...], axis=1, keepdims=True)
        mom_ref[...] = jnp.sum(mo_sc[...], axis=1, keepdims=True)
        pick_ref[...] = jnp.sum(p_sc[...], axis=1, keepdims=True)


def fused_stats(normed, piece, bias, vocab_ids, ids, tm=512, tn=512):
    rows, depth = normed.shape
    cols = piece.shape[0]
    grid = (rows // tm, cols // tn)
    stat = jax.ShapeDtypeStruct((rows, 1), jnp.float32)
    stat_spec = pl.BlockSpec((tm, 1), lambda i, j: (i, 0))
    return pl.pallas_call(
        functools.partial(stats_kernel, grid[1]),
        out_shape=(stat, stat, stat, stat),
        grid=grid,
        in_specs=[
            pl.BlockSpec((tm, depth), lambda i, j: (i, 0)),
            pl.BlockSpec((tn, depth), lambda i, j: (j, 0)),
            pl.BlockSpec((1, tn), lambda i, j: (0, j)),
            pl.BlockSpec((1, tn), lambda i, j: (0, j)),
            pl.BlockSpec((tm, 1), lambda i, j: (i, 0)),
        ],
        out_specs=(stat_spec, stat_spec, stat_spec, stat_spec),
        scratch_shapes=[pltpu.VMEM((tm, 1), jnp.float32)] + [pltpu.VMEM((tm, LANES), jnp.float32)] * 3,
        compiler_params=pltpu.CompilerParams(dimension_semantics=("arbitrary", "arbitrary")),
        cost_estimate=pl.CostEstimate(
            flops=2 * rows * cols * depth,
            transcendentals=rows * cols,
            bytes_accessed=2 * (rows * depth + grid[0] * cols * depth),
        ),
    )(normed, piece, bias, vocab_ids, ids)


def chunk_stats(normed, piece, valid, vocab_ids, ids):
    bias = jnp.where(valid, 0.0, NEG).astype(jnp.float32)[None, :]
    top, total, moment, pick = fused_stats(normed, piece, bias, vocab_ids[None, :], ids[:, None])
    return top[:, 0], total[:, 0], moment[:, 0], pick[:, 0]


def merge(stats):
    tops = jnp.stack([s[0] for s in stats])
    top = jnp.max(tops, axis=0)
    factor = jnp.exp(tops - top[None, :])
    total = jnp.sum(factor * jnp.stack([s[1] for s in stats]), axis=0)
    moment = jnp.sum(factor * jnp.stack([s[2] for s in stats]), axis=0)
    pick = jnp.sum(jnp.stack([s[3] for s in stats]), axis=0)
    return top, total, moment, pick


def body(hidden, gain, head, token_ids, lengths, prompt_of):
    rows, part_width = hidden.shape
    splits = lax.axis_size("x")
    column_index = lax.axis_index("x")
    req_count = lax.axis_size(REQ)
    shard_cols = head.shape[1]
    width = part_width * splits

    extra = jnp.zeros((8, part_width), hidden.dtype).at[0].set(gain)
    packed = jnp.concatenate([hidden, extra], axis=0)
    shift = lambda x, d: lax.ppermute(x, "x", [(i, (i + d) % splits) for i in range(splits)])
    from_left = shift(packed, 1)
    from_right = shift(packed, -1)
    from_far = shift(from_left, 1)
    stacked = jnp.stack([packed, from_right, from_far, from_left])
    order = (jnp.arange(splits, dtype=jnp.int32) - column_index) % splits
    stacked = jnp.take(stacked, order, axis=0)
    gathered = jnp.transpose(stacked, (1, 0, 2)).reshape(rows + 8, width)
    widened = gathered[:rows].astype(jnp.float32)
    gain_full = gathered[rows].astype(jnp.float32)
    scale = lax.rsqrt(jnp.sum(widened * widened, axis=1) / width + eps)
    normed = (widened * scale[:, None] * gain_full[None, :]).astype(jnp.bfloat16)

    chunk = 256
    bounds = [(lo, min(lo + chunk, shard_cols)) for lo in range(0, shard_cols, chunk)]
    stats = []
    for lo, hi in bounds:
        part = head[:, lo:hi].T
        if hi - lo < chunk:
            part = jnp.concatenate([part, jnp.zeros((chunk - (hi - lo), part.shape[1]), part.dtype)], axis=0)
        part = with_layout_constraint(part, Layout(major_to_minor=(0, 1)))
        piece = lax.all_gather(part, REQ, axis=0, tiled=False)
        piece = with_layout_constraint(piece, Layout(major_to_minor=(0, 1, 2)))
        piece = piece.reshape(req_count * chunk, piece.shape[2])
        g = jnp.arange(req_count * chunk, dtype=jnp.int32)
        owner = g // chunk
        offset = lo + g % chunk
        valid = offset < hi
        vocab_ids = jnp.where(valid, (owner * splits + column_index) * shard_cols + offset, -1)
        stats.append(chunk_stats(normed, piece, valid, vocab_ids, token_ids))
    mine = merge(stats)

    everyone = lax.all_gather(jnp.stack(mine), "x", axis=0, tiled=False)
    top, total, moment, picked = merge([tuple(everyone[k, j] for j in range(4)) for k in range(splits)])

    positions = jnp.arange(rows, dtype=jnp.int32)
    live = positions < lengths[0]
    safe_total = jnp.where(live, total, 1.0)
    log_norm = top + jnp.log(safe_total)
    logprob = jnp.where(live, picked - log_norm, 0.0)
    entropy = jnp.where(live, log_norm - moment / safe_total, 0.0)
    onehot = (jnp.arange(PROMPTS, dtype=jnp.int32) == prompt_of[0]).astype(jnp.float32)
    share = rows // splits
    own_logprob = lax.dynamic_slice_in_dim(logprob, column_index * share, share)
    own_entropy = lax.dynamic_slice_in_dim(entropy, column_index * share, share)
    summary = jnp.stack([jnp.sum(entropy), jnp.sum(logprob), lengths[0].astype(jnp.float32)])
    summed = onehot[:, None] * summary[None, :]
    for name in REQ[::-1]:
        summed = lax.psum(summed, name)
    prompt_stats = summed[:, :2] / jnp.maximum(summed[:, 2:3], 1.0)
    return (own_logprob, own_entropy, prompt_stats)


def solution(mesh):
    req_axes = mesh.devices.shape[0] // 8
    fine = Mesh(mesh.devices.reshape(req_axes, 4, 2, mesh.devices.shape[1]), ("y", "z", "c", "x"))
    in_specs = (
        P(REQ, "x"),
        P("x"),
        P(None, REQ + ("x",)),
        P(REQ),
        P(REQ),
        P(REQ),
    )
    out_specs = (P(REQ + ("x",)), P(REQ + ("x",)), P())
    return jax.shard_map(body, mesh=fine, in_specs=in_specs, out_specs=out_specs, check_vma=False)
```

```python
import functools

import jax
import jax.numpy as jnp
from jax import lax
from jax.experimental import pallas as pl
from jax.experimental.pallas import tpu as pltpu
from jax.sharding import Mesh, PartitionSpec as P
from jax.experimental.layout import Layout, with_layout_constraint

PROMPTS = 4
REQ = ("y", "z", "c")
NEG = -1e30
SUB = 8

eps = 1e-06


def stats_kernel(steps, w_ref, x_ref, b_ref, v_ref, t_ref, top_ref, tot_ref, mom_ref, pick_ref, m_sc, s_sc, mo_sc, p_sc):
    j = pl.program_id(1)

    @pl.when(j == 0)
    def _():
        m_sc[...] = jnp.full(m_sc.shape, NEG, jnp.float32)
        s_sc[...] = jnp.zeros(s_sc.shape, jnp.float32)
        mo_sc[...] = jnp.zeros(mo_sc.shape, jnp.float32)
        p_sc[...] = jnp.zeros(p_sc.shape, jnp.float32)

    logits = jnp.dot(w_ref[...], x_ref[...], preferred_element_type=jnp.float32)
    logits = logits + b_ref[...]
    tn, tm = logits.shape
    grouped = logits.reshape(tn // SUB, SUB, tm)
    m_old = m_sc[...]
    m_new = jnp.maximum(m_old, jnp.max(jnp.max(grouped, axis=0), axis=0, keepdims=True))
    alpha = jnp.exp(m_old - m_new)
    e = jnp.exp(logits - m_new)
    hit = jnp.where(v_ref[...] == t_ref[...], logits, 0.0)
    s_sc[...] = s_sc[...] * alpha + jnp.sum(e.reshape(tn // SUB, SUB, tm), axis=0)
    mo_sc[...] = mo_sc[...] * alpha + jnp.sum((e * logits).reshape(tn // SUB, SUB, tm), axis=0)
    p_sc[...] = p_sc[...] + jnp.sum(hit.reshape(tn // SUB, SUB, tm), axis=0)
    m_sc[...] = m_new

    @pl.when(j == steps - 1)
    def _():
        top_ref[...] = m_sc[...]
        tot_ref[...] = jnp.sum(s_sc[...], axis=0, keepdims=True)
        mom_ref[...] = jnp.sum(mo_sc[...], axis=0, keepdims=True)
        pick_ref[...] = jnp.sum(p_sc[...], axis=0, keepdims=True)


def fused_stats(normed_t, piece, bias, vocab_ids, ids, tm=1024, tn=256):
    depth, rows = normed_t.shape
    cols = piece.shape[0]
    grid = (rows // tm, cols // tn)
    stat = jax.ShapeDtypeStruct((1, rows), jnp.float32)
    stat_spec = pl.BlockSpec((1, tm), lambda i, j: (0, i))
    return pl.pallas_call(
        functools.partial(stats_kernel, grid[1]),
        out_shape=(stat, stat, stat, stat),
        grid=grid,
        in_specs=[
            pl.BlockSpec((tn, depth), lambda i, j: (j, 0)),
            pl.BlockSpec((depth, tm), lambda i, j: (0, i)),
            pl.BlockSpec((tn, 1), lambda i, j: (j, 0)),
            pl.BlockSpec((tn, 1), lambda i, j: (j, 0)),
            pl.BlockSpec((1, tm), lambda i, j: (0, i)),
        ],
        out_specs=(stat_spec, stat_spec, stat_spec, stat_spec),
        scratch_shapes=[pltpu.VMEM((1, tm), jnp.float32)] + [pltpu.VMEM((SUB, tm), jnp.float32)] * 3,
        compiler_params=pltpu.CompilerParams(dimension_semantics=("arbitrary", "arbitrary")),
        cost_estimate=pl.CostEstimate(
            flops=2 * rows * cols * depth,
            transcendentals=rows * cols,
            bytes_accessed=2 * (rows * depth + grid[0] * cols * depth),
        ),
    )(piece, normed_t, bias, vocab_ids, ids)


def chunk_stats(normed, piece, valid, vocab_ids, ids):
    bias = jnp.where(valid, 0.0, NEG).astype(jnp.float32)[:, None]
    top, total, moment, pick = fused_stats(normed.T, piece, bias, vocab_ids[:, None], ids[None, :])
    return top[0], total[0], moment[0], pick[0]


def merge(stats):
    tops = jnp.stack([s[0] for s in stats])
    top = jnp.max(tops, axis=0)
    factor = jnp.exp(tops - top[None, :])
    total = jnp.sum(factor * jnp.stack([s[1] for s in stats]), axis=0)
    moment = jnp.sum(factor * jnp.stack([s[2] for s in stats]), axis=0)
    pick = jnp.sum(jnp.stack([s[3] for s in stats]), axis=0)
    return top, total, moment, pick


def body(hidden, gain, head, token_ids, lengths, prompt_of):
    rows, part_width = hidden.shape
    splits = lax.axis_size("x")
    column_index = lax.axis_index("x")
    req_count = lax.axis_size(REQ)
    shard_cols = head.shape[1]
    width = part_width * splits

    extra = jnp.zeros((8, part_width), hidden.dtype).at[0].set(gain)
    packed = jnp.concatenate([hidden, extra], axis=0)
    shift = lambda x, d: lax.ppermute(x, "x", [(i, (i + d) % splits) for i in range(splits)])
    from_left = shift(packed, 1)
    from_right = shift(packed, -1)
    from_far = shift(from_left, 1)
    stacked = jnp.stack([packed, from_right, from_far, from_left])
    order = (jnp.arange(splits, dtype=jnp.int32) - column_index) % splits
    stacked = jnp.take(stacked, order, axis=0)
    gathered = jnp.transpose(stacked, (1, 0, 2)).reshape(rows + 8, width)
    widened = gathered[:rows].astype(jnp.float32)
    gain_full = gathered[rows].astype(jnp.float32)
    scale = lax.rsqrt(jnp.sum(widened * widened, axis=1) / width + eps)
    normed = (widened * scale[:, None] * gain_full[None, :]).astype(jnp.bfloat16)

    chunk = 256
    bounds = [(lo, min(lo + chunk, shard_cols)) for lo in range(0, shard_cols, chunk)]
    stats = []
    for lo, hi in bounds:
        part = head[:, lo:hi].T
        if hi - lo < chunk:
            part = jnp.concatenate([part, jnp.zeros((chunk - (hi - lo), part.shape[1]), part.dtype)], axis=0)
        part = with_layout_constraint(part, Layout(major_to_minor=(0, 1)))
        piece = lax.all_gather(part, REQ, axis=0, tiled=False)
        piece = with_layout_constraint(piece, Layout(major_to_minor=(0, 1, 2)))
        piece = piece.reshape(req_count * chunk, piece.shape[2])
        g = jnp.arange(req_count * chunk, dtype=jnp.int32)
        owner = g // chunk
        offset = lo + g % chunk
        valid = offset < hi
        vocab_ids = jnp.where(valid, (owner * splits + column_index) * shard_cols + offset, -1)
        stats.append(chunk_stats(normed, piece, valid, vocab_ids, token_ids))
    mine = merge(stats)

    everyone = lax.all_gather(jnp.stack(mine), "x", axis=0, tiled=False)
    top, total, moment, picked = merge([tuple(everyone[k, j] for j in range(4)) for k in range(splits)])

    positions = jnp.arange(rows, dtype=jnp.int32)
    live = positions < lengths[0]
    safe_total = jnp.where(live, total, 1.0)
    log_norm = top + jnp.log(safe_total)
    logprob = jnp.where(live, picked - log_norm, 0.0)
    entropy = jnp.where(live, log_norm - moment / safe_total, 0.0)
    onehot = (jnp.arange(PROMPTS, dtype=jnp.int32) == prompt_of[0]).astype(jnp.float32)
    share = rows // splits
    own_logprob = lax.dynamic_slice_in_dim(logprob, column_index * share, share)
    own_entropy = lax.dynamic_slice_in_dim(entropy, column_index * share, share)
    summary = jnp.stack([jnp.sum(entropy), jnp.sum(logprob), lengths[0].astype(jnp.float32)])
    summed = onehot[:, None] * summary[None, :]
    for name in REQ[::-1]:
        summed = lax.psum(summed, name)
    prompt_stats = summed[:, :2] / jnp.maximum(summed[:, 2:3], 1.0)
    return (own_logprob, own_entropy, prompt_stats)


def solution(mesh):
    req_axes = mesh.devices.shape[0] // 8
    fine = Mesh(mesh.devices.reshape(req_axes, 4, 2, mesh.devices.shape[1]), ("y", "z", "c", "x"))
    in_specs = (
        P(REQ, "x"),
        P("x"),
        P(None, REQ + ("x",)),
        P(REQ),
        P(REQ),
        P(REQ),
    )
    out_specs = (P(REQ + ("x",)), P(REQ + ("x",)), P())
    return jax.shard_map(body, mesh=fine, in_specs=in_specs, out_specs=out_specs, check_vma=False)
```

```python
import functools

import jax
import jax.numpy as jnp
from jax import lax
from jax.experimental import pallas as pl
from jax.experimental.pallas import tpu as pltpu
from jax.sharding import Mesh, PartitionSpec as P
from jax.experimental.layout import Layout, with_layout_constraint

PROMPTS = 4
REQ = ("y", "z", "c")
MESH_AXES = ("y", "z", "c", "x")
NEG = -1e30
SUB = 8

eps = 1e-06


def peer_kernel(n, coords_of, x_ref, o_ref, held, send_sem, recv_sem):
    me, coords = coords_of()
    barrier = pltpu.get_barrier_semaphore()
    for d in range(1, n):
        pl.semaphore_signal(barrier, inc=1, device_id=coords((me + d) % n), device_id_type=pl.DeviceIdType.MESH)
    pl.semaphore_wait(barrier, n - 1)
    held[pl.ds(me, 1)] = x_ref[...][None]
    copies = []
    for d in range(1, n):
        c = pltpu.make_async_remote_copy(
            src_ref=x_ref, dst_ref=held.at[me], send_sem=send_sem.at[d], recv_sem=recv_sem.at[d],
            device_id=coords((me + d) % n), device_id_type=pl.DeviceIdType.MESH)
        c.start()
        copies.append(c)
    for c in copies:
        c.wait()
    o_ref[...] = held[...]


def peer_gather(x, n, coords_of, cid):
    return pl.pallas_call(
        functools.partial(peer_kernel, n, coords_of),
        out_shape=jax.ShapeDtypeStruct((n,) + x.shape, x.dtype),
        in_specs=[pl.BlockSpec(memory_space=pltpu.VMEM)],
        out_specs=pl.BlockSpec(memory_space=pltpu.VMEM),
        scratch_shapes=[pltpu.VMEM((n,) + x.shape, x.dtype), pltpu.SemaphoreType.DMA((n,)), pltpu.SemaphoreType.DMA((n,))],
        compiler_params=pltpu.CompilerParams(collective_id=cid, has_side_effects=True),
    )(x)


def bulk_kernel(n, coords_of, x_ref, o_ref, send_sem, recv_sem, own_sem):
    me, coords = coords_of()
    barrier = pltpu.get_barrier_semaphore()
    for d in range(1, n):
        pl.semaphore_signal(barrier, inc=1, device_id=coords((me + d) % n), device_id_type=pl.DeviceIdType.MESH)
    pl.semaphore_wait(barrier, n - 1)
    own = pltpu.make_async_copy(x_ref, o_ref.at[me], own_sem)
    own.start()
    copies = []
    for d in range(1, n):
        c = pltpu.make_async_remote_copy(
            src_ref=x_ref, dst_ref=o_ref.at[me], send_sem=send_sem.at[d], recv_sem=recv_sem.at[d],
            device_id=coords((me + d) % n), device_id_type=pl.DeviceIdType.MESH)
        c.start()
        copies.append(c)
    own.wait()
    for c in copies:
        c.wait()


def bulk_gather(x, n, coords_of, cid):
    return pl.pallas_call(
        functools.partial(bulk_kernel, n, coords_of),
        out_shape=jax.ShapeDtypeStruct((n,) + x.shape, x.dtype),
        in_specs=[pl.BlockSpec(memory_space=pl.ANY)],
        out_specs=pl.BlockSpec(memory_space=pl.ANY),
        scratch_shapes=[pltpu.SemaphoreType.DMA((n,)), pltpu.SemaphoreType.DMA((n,)), pltpu.SemaphoreType.DMA(())],
        compiler_params=pltpu.CompilerParams(collective_id=cid, has_side_effects=True),
    )(x)


def along_x():
    here = tuple(lax.axis_index(name) for name in MESH_AXES)
    return here[3], lambda t: here[:3] + (t,)


def along_req():
    here = tuple(lax.axis_index(name) for name in MESH_AXES)
    zs, cs = lax.axis_size("z"), lax.axis_size("c")
    me = (here[0] * zs + here[1]) * cs + here[2]
    return me, lambda t: (t // (zs * cs), (t // cs) % zs, t % cs, here[3])


def stats_kernel(steps, w_ref, x_ref, b_ref, v_ref, t_ref, top_ref, tot_ref, mom_ref, pick_ref, m_sc, s_sc, mo_sc, p_sc):
    j = pl.program_id(1)

    @pl.when(j == 0)
    def _():
        m_sc[...] = jnp.full(m_sc.shape, NEG, jnp.float32)
        s_sc[...] = jnp.zeros(s_sc.shape, jnp.float32)
        mo_sc[...] = jnp.zeros(mo_sc.shape, jnp.float32)
        p_sc[...] = jnp.zeros(p_sc.shape, jnp.float32)

    logits = jnp.dot(w_ref[...], x_ref[...], preferred_element_type=jnp.float32)
    logits = logits + b_ref[...]
    tn, tm = logits.shape
    grouped = logits.reshape(tn // SUB, SUB, tm)
    m_old = m_sc[...]
    m_new = jnp.maximum(m_old, jnp.max(jnp.max(grouped, axis=0), axis=0, keepdims=True))
    alpha = jnp.exp(m_old - m_new)
    e = jnp.exp(logits - m_new)
    hit = jnp.where(v_ref[...] == t_ref[...], logits, 0.0)
    s_sc[...] = s_sc[...] * alpha + jnp.sum(e.reshape(tn // SUB, SUB, tm), axis=0)
    mo_sc[...] = mo_sc[...] * alpha + jnp.sum((e * logits).reshape(tn // SUB, SUB, tm), axis=0)
    p_sc[...] = p_sc[...] + jnp.sum(hit.reshape(tn // SUB, SUB, tm), axis=0)
    m_sc[...] = m_new

    @pl.when(j == steps - 1)
    def _():
        top_ref[...] = m_sc[...]
        tot_ref[...] = jnp.sum(s_sc[...], axis=0, keepdims=True)
        mom_ref[...] = jnp.sum(mo_sc[...], axis=0, keepdims=True)
        pick_ref[...] = jnp.sum(p_sc[...], axis=0, keepdims=True)


def fused_stats(normed_t, piece, bias, vocab_ids, ids, tm=1024, tn=256):
    depth, rows = normed_t.shape
    cols = piece.shape[0]
    grid = (rows // tm, cols // tn)
    stat = jax.ShapeDtypeStruct((1, rows), jnp.float32)
    stat_spec = pl.BlockSpec((1, tm), lambda i, j: (0, i))
    return pl.pallas_call(
        functools.partial(stats_kernel, grid[1]),
        out_shape=(stat, stat, stat, stat),
        grid=grid,
        in_specs=[
            pl.BlockSpec((tn, depth), lambda i, j: (j, 0)),
            pl.BlockSpec((depth, tm), lambda i, j: (0, i)),
            pl.BlockSpec((tn, 1), lambda i, j: (j, 0)),
            pl.BlockSpec((tn, 1), lambda i, j: (j, 0)),
            pl.BlockSpec((1, tm), lambda i, j: (0, i)),
        ],
        out_specs=(stat_spec, stat_spec, stat_spec, stat_spec),
        scratch_shapes=[pltpu.VMEM((1, tm), jnp.float32)] + [pltpu.VMEM((SUB, tm), jnp.float32)] * 3,
        compiler_params=pltpu.CompilerParams(dimension_semantics=("arbitrary", "arbitrary")),
        cost_estimate=pl.CostEstimate(
            flops=2 * rows * cols * depth,
            transcendentals=rows * cols,
            bytes_accessed=2 * (rows * depth + grid[0] * cols * depth),
        ),
    )(piece, normed_t, bias, vocab_ids, ids)


def chunk_stats(normed, piece, valid, vocab_ids, ids):
    bias = jnp.where(valid, 0.0, NEG).astype(jnp.float32)[:, None]
    top, total, moment, pick = fused_stats(normed.T, piece, bias, vocab_ids[:, None], ids[None, :])
    return top[0], total[0], moment[0], pick[0]


def merge(stats):
    tops = jnp.stack([s[0] for s in stats])
    top = jnp.max(tops, axis=0)
    factor = jnp.exp(tops - top[None, :])
    total = jnp.sum(factor * jnp.stack([s[1] for s in stats]), axis=0)
    moment = jnp.sum(factor * jnp.stack([s[2] for s in stats]), axis=0)
    pick = jnp.sum(jnp.stack([s[3] for s in stats]), axis=0)
    return top, total, moment, pick


def body(hidden, gain, head, token_ids, lengths, prompt_of):
    rows, part_width = hidden.shape
    splits = lax.axis_size("x")
    column_index = lax.axis_index("x")
    req_count = lax.axis_size(REQ)
    shard_cols = head.shape[1]
    width = part_width * splits

    extra = jnp.zeros((8, part_width), hidden.dtype).at[0].set(gain)
    packed = jnp.concatenate([hidden, extra], axis=0)
    shift = lambda x, d: lax.ppermute(x, "x", [(i, (i + d) % splits) for i in range(splits)])
    from_left = shift(packed, 1)
    from_right = shift(packed, -1)
    from_far = shift(from_left, 1)
    stacked = jnp.stack([packed, from_right, from_far, from_left])
    order = (jnp.arange(splits, dtype=jnp.int32) - column_index) % splits
    stacked = jnp.take(stacked, order, axis=0)
    gathered = jnp.transpose(stacked, (1, 0, 2)).reshape(rows + 8, width)
    widened = gathered[:rows].astype(jnp.float32)
    gain_full = gathered[rows].astype(jnp.float32)
    scale = lax.rsqrt(jnp.sum(widened * widened, axis=1) / width + eps)
    normed = (widened * scale[:, None] * gain_full[None, :]).astype(jnp.bfloat16)

    chunk = 256
    half = chunk // 2
    part = head.T
    part = jnp.concatenate([part, jnp.zeros((chunk - shard_cols, part.shape[1]), part.dtype)], axis=0)
    part = with_layout_constraint(part, Layout(major_to_minor=(0, 1)))
    stats = []
    for lo in (0, half):
        hi = min(lo + half, shard_cols)
        sub = part[lo:lo + half]
        if lo == 0:
            piece = lax.all_gather(sub, REQ, axis=0, tiled=False)
            piece = with_layout_constraint(piece, Layout(major_to_minor=(0, 1, 2)))
        else:
            piece = bulk_gather(sub, req_count, along_req, 2)
        piece = piece.reshape(req_count * half, piece.shape[2])
        g = jnp.arange(req_count * half, dtype=jnp.int32)
        owner = g // half
        offset = lo + g % half
        valid = offset < hi
        vocab_ids = jnp.where(valid, (owner * splits + column_index) * shard_cols + offset, -1)
        stats.append(chunk_stats(normed, piece, valid, vocab_ids, token_ids))
    mine = merge(stats)

    everyone = peer_gather(jnp.stack(mine), splits, along_x, 0)
    top, total, moment, picked = merge([tuple(everyone[k, j] for j in range(4)) for k in range(splits)])

    positions = jnp.arange(rows, dtype=jnp.int32)
    live = positions < lengths[0]
    safe_total = jnp.where(live, total, 1.0)
    log_norm = top + jnp.log(safe_total)
    logprob = jnp.where(live, picked - log_norm, 0.0)
    entropy = jnp.where(live, log_norm - moment / safe_total, 0.0)
    onehot = (jnp.arange(PROMPTS, dtype=jnp.int32) == prompt_of[0]).astype(jnp.float32)
    share = rows // splits
    own_logprob = lax.dynamic_slice_in_dim(logprob, column_index * share, share)
    own_entropy = lax.dynamic_slice_in_dim(entropy, column_index * share, share)
    summary = jnp.stack([jnp.sum(entropy), jnp.sum(logprob), lengths[0].astype(jnp.float32)])
    summed = jnp.zeros((8, 128), jnp.float32).at[:PROMPTS, :3].set(onehot[:, None] * summary[None, :])
    summed = jnp.sum(peer_gather(summed, req_count, along_req, 1), axis=0)[:PROMPTS, :3]
    prompt_stats = summed[:, :2] / jnp.maximum(summed[:, 2:3], 1.0)
    return (own_logprob, own_entropy, prompt_stats)


def solution(mesh):
    req_axes = mesh.devices.shape[0] // 8
    fine = Mesh(mesh.devices.reshape(req_axes, 4, 2, mesh.devices.shape[1]), ("y", "z", "c", "x"))
    in_specs = (
        P(REQ, "x"),
        P("x"),
        P(None, REQ + ("x",)),
        P(REQ),
        P(REQ),
        P(REQ),
    )
    out_specs = (P(REQ + ("x",)), P(REQ + ("x",)), P())
    return jax.shard_map(body, mesh=fine, in_specs=in_specs, out_specs=out_specs, check_vma=False)
```

```python
import functools

import jax
import jax.numpy as jnp
from jax import lax
from jax.experimental import pallas as pl
from jax.experimental.pallas import tpu as pltpu
from jax.sharding import Mesh, PartitionSpec as P
from jax.experimental.layout import Layout, with_layout_constraint

PROMPTS = 4
REQ = ("y", "z", "c")
MESH_AXES = ("y", "z", "c", "x")
NEG = -1e30
SUB = 8

eps = 1e-06


def peer_kernel(n, coords_of, x_ref, o_ref, held, send_sem, recv_sem):
    me, coords = coords_of()
    barrier = pltpu.get_barrier_semaphore()
    for d in range(1, n):
        pl.semaphore_signal(barrier, inc=1, device_id=coords((me + d) % n), device_id_type=pl.DeviceIdType.MESH)
    pl.semaphore_wait(barrier, n - 1)
    held[pl.ds(me, 1)] = x_ref[...][None]
    copies = []
    for d in range(1, n):
        c = pltpu.make_async_remote_copy(
            src_ref=x_ref, dst_ref=held.at[me], send_sem=send_sem.at[d], recv_sem=recv_sem.at[d],
            device_id=coords((me + d) % n), device_id_type=pl.DeviceIdType.MESH)
        c.start()
        copies.append(c)
    for c in copies:
        c.wait()
    o_ref[...] = held[...]


def peer_gather(x, n, coords_of, cid):
    return pl.pallas_call(
        functools.partial(peer_kernel, n, coords_of),
        out_shape=jax.ShapeDtypeStruct((n,) + x.shape, x.dtype),
        in_specs=[pl.BlockSpec(memory_space=pltpu.VMEM)],
        out_specs=pl.BlockSpec(memory_space=pltpu.VMEM),
        scratch_shapes=[pltpu.VMEM((n,) + x.shape, x.dtype), pltpu.SemaphoreType.DMA((n,)), pltpu.SemaphoreType.DMA((n,))],
        compiler_params=pltpu.CompilerParams(collective_id=cid, has_side_effects=True),
    )(x)


def along_x():
    here = tuple(lax.axis_index(name) for name in MESH_AXES)
    return here[3], lambda t: here[:3] + (t,)


def along_req():
    here = tuple(lax.axis_index(name) for name in MESH_AXES)
    zs, cs = lax.axis_size("z"), lax.axis_size("c")
    me = (here[0] * zs + here[1]) * cs + here[2]
    return me, lambda t: (t // (zs * cs), (t // cs) % zs, t % cs, here[3])


def stats_kernel(steps, w_ref, x_ref, b_ref, v_ref, t_ref, top_ref, tot_ref, mom_ref, pick_ref, m_sc, s_sc, mo_sc, p_sc):
    j = pl.program_id(1)

    @pl.when(j == 0)
    def _():
        m_sc[...] = jnp.full(m_sc.shape, NEG, jnp.float32)
        s_sc[...] = jnp.zeros(s_sc.shape, jnp.float32)
        mo_sc[...] = jnp.zeros(mo_sc.shape, jnp.float32)
        p_sc[...] = jnp.zeros(p_sc.shape, jnp.float32)

    logits = jnp.dot(w_ref[...], x_ref[...], preferred_element_type=jnp.float32)
    logits = logits + b_ref[...]
    tn, tm = logits.shape
    grouped = logits.reshape(tn // SUB, SUB, tm)
    m_old = m_sc[...]
    m_new = jnp.maximum(m_old, jnp.max(jnp.max(grouped, axis=0), axis=0, keepdims=True))
    alpha = jnp.exp(m_old - m_new)
    e = jnp.exp(logits - m_new)
    hit = jnp.where(v_ref[...] == t_ref[...], logits, 0.0)
    s_sc[...] = s_sc[...] * alpha + jnp.sum(e.reshape(tn // SUB, SUB, tm), axis=0)
    mo_sc[...] = mo_sc[...] * alpha + jnp.sum((e * logits).reshape(tn // SUB, SUB, tm), axis=0)
    p_sc[...] = p_sc[...] + jnp.sum(hit.reshape(tn // SUB, SUB, tm), axis=0)
    m_sc[...] = m_new

    @pl.when(j == steps - 1)
    def _():
        top_ref[...] = m_sc[...]
        tot_ref[...] = jnp.sum(s_sc[...], axis=0, keepdims=True)
        mom_ref[...] = jnp.sum(mo_sc[...], axis=0, keepdims=True)
        pick_ref[...] = jnp.sum(p_sc[...], axis=0, keepdims=True)


def fused_stats(normed_t, piece, bias, vocab_ids, ids, tm=1024, tn=1024):
    depth, rows = normed_t.shape
    cols = piece.shape[0]
    grid = (rows // tm, cols // tn)
    stat = jax.ShapeDtypeStruct((1, rows), jnp.float32)
    stat_spec = pl.BlockSpec((1, tm), lambda i, j: (0, i))
    return pl.pallas_call(
        functools.partial(stats_kernel, grid[1]),
        out_shape=(stat, stat, stat, stat),
        grid=grid,
        in_specs=[
            pl.BlockSpec((tn, depth), lambda i, j: (j, 0)),
            pl.BlockSpec((depth, tm), lambda i, j: (0, i)),
            pl.BlockSpec((tn, 1), lambda i, j: (j, 0)),
            pl.BlockSpec((tn, 1), lambda i, j: (j, 0)),
            pl.BlockSpec((1, tm), lambda i, j: (0, i)),
        ],
        out_specs=(stat_spec, stat_spec, stat_spec, stat_spec),
        scratch_shapes=[pltpu.VMEM((1, tm), jnp.float32)] + [pltpu.VMEM((SUB, tm), jnp.float32)] * 3,
        compiler_params=pltpu.CompilerParams(dimension_semantics=("arbitrary", "arbitrary")),
        cost_estimate=pl.CostEstimate(
            flops=2 * rows * cols * depth,
            transcendentals=rows * cols,
            bytes_accessed=2 * (rows * depth + grid[0] * cols * depth),
        ),
    )(piece, normed_t, bias, vocab_ids, ids)


def chunk_stats(normed, piece, valid, vocab_ids, ids):
    bias = jnp.where(valid, 0.0, NEG).astype(jnp.float32)[:, None]
    top, total, moment, pick = fused_stats(normed.T, piece, bias, vocab_ids[:, None], ids[None, :])
    return top[0], total[0], moment[0], pick[0]


def merge(stats):
    tops = jnp.stack([s[0] for s in stats])
    top = jnp.max(tops, axis=0)
    factor = jnp.exp(tops - top[None, :])
    total = jnp.sum(factor * jnp.stack([s[1] for s in stats]), axis=0)
    moment = jnp.sum(factor * jnp.stack([s[2] for s in stats]), axis=0)
    pick = jnp.sum(jnp.stack([s[3] for s in stats]), axis=0)
    return top, total, moment, pick


def body(hidden, gain, head, token_ids, lengths, prompt_of):
    rows, part_width = hidden.shape
    splits = lax.axis_size("x")
    column_index = lax.axis_index("x")
    req_count = lax.axis_size(REQ)
    shard_cols = head.shape[1]
    width = part_width * splits

    extra = jnp.zeros((8, part_width), hidden.dtype).at[0].set(gain)
    packed = jnp.concatenate([hidden, extra], axis=0)
    shift = lambda x, d: lax.ppermute(x, "x", [(i, (i + d) % splits) for i in range(splits)])
    from_left = shift(packed, 1)
    from_right = shift(packed, -1)
    from_far = shift(from_left, 1)
    stacked = jnp.stack([packed, from_right, from_far, from_left])
    order = (jnp.arange(splits, dtype=jnp.int32) - column_index) % splits
    stacked = jnp.take(stacked, order, axis=0)
    gathered = jnp.transpose(stacked, (1, 0, 2)).reshape(rows + 8, width)
    widened = gathered[:rows].astype(jnp.float32)
    gain_full = gathered[rows].astype(jnp.float32)
    scale = lax.rsqrt(jnp.sum(widened * widened, axis=1) / width + eps)
    normed = (widened * scale[:, None] * gain_full[None, :]).astype(jnp.bfloat16)

    chunk = 256
    bounds = [(lo, min(lo + chunk, shard_cols)) for lo in range(0, shard_cols, chunk)]
    stats = []
    for lo, hi in bounds:
        part = head[:, lo:hi].T
        if hi - lo < chunk:
            part = jnp.concatenate([part, jnp.zeros((chunk - (hi - lo), part.shape[1]), part.dtype)], axis=0)
        part = with_layout_constraint(part, Layout(major_to_minor=(0, 1)))
        piece = lax.all_gather(part, REQ, axis=0, tiled=False)
        piece = with_layout_constraint(piece, Layout(major_to_minor=(0, 1, 2)))
        piece = piece.reshape(req_count * chunk, piece.shape[2])
        g = jnp.arange(req_count * chunk, dtype=jnp.int32)
        owner = g // chunk
        offset = lo + g % chunk
        valid = offset < hi
        vocab_ids = jnp.where(valid, (owner * splits + column_index) * shard_cols + offset, -1)
        stats.append(chunk_stats(normed, piece, valid, vocab_ids, token_ids))
    mine = merge(stats)

    everyone = peer_gather(jnp.stack(mine), splits, along_x, 0)
    top, total, moment, picked = merge([tuple(everyone[k, j] for j in range(4)) for k in range(splits)])

    positions = jnp.arange(rows, dtype=jnp.int32)
    live = positions < lengths[0]
    safe_total = jnp.where(live, total, 1.0)
    log_norm = top + jnp.log(safe_total)
    logprob = jnp.where(live, picked - log_norm, 0.0)
    entropy = jnp.where(live, log_norm - moment / safe_total, 0.0)
    onehot = (jnp.arange(PROMPTS, dtype=jnp.int32) == prompt_of[0]).astype(jnp.float32)
    share = rows // splits
    own_logprob = lax.dynamic_slice_in_dim(logprob, column_index * share, share)
    own_entropy = lax.dynamic_slice_in_dim(entropy, column_index * share, share)
    summary = jnp.stack([jnp.sum(entropy), jnp.sum(logprob), lengths[0].astype(jnp.float32)])
    summed = jnp.zeros((8, 128), jnp.float32).at[:PROMPTS, :3].set(onehot[:, None] * summary[None, :])
    summed = jnp.sum(peer_gather(summed, req_count, along_req, 1), axis=0)[:PROMPTS, :3]
    prompt_stats = summed[:, :2] / jnp.maximum(summed[:, 2:3], 1.0)
    return (own_logprob, own_entropy, prompt_stats)


def solution(mesh):
    req_axes = mesh.devices.shape[0] // 8
    fine = Mesh(mesh.devices.reshape(req_axes, 4, 2, mesh.devices.shape[1]), ("y", "z", "c", "x"))
    in_specs = (
        P(REQ, "x"),
        P("x"),
        P(None, REQ + ("x",)),
        P(REQ),
        P(REQ),
        P(REQ),
    )
    out_specs = (P(REQ + ("x",)), P(REQ + ("x",)), P())
    return jax.shard_map(body, mesh=fine, in_specs=in_specs, out_specs=out_specs, check_vma=False)
```

```python
import functools

import jax
import jax.numpy as jnp
from jax import lax
from jax.experimental import pallas as pl
from jax.experimental.pallas import tpu as pltpu
from jax.sharding import Mesh, PartitionSpec as P
from jax.experimental.layout import Layout, with_layout_constraint

PROMPTS = 4
REQ = ("y", "z", "c")
MESH_AXES = ("y", "z", "c", "x")
NEG = -1e30
SUB = 8

eps = 1e-06


def peer_kernel(n, coords_of, x_ref, o_ref, held, send_sem, recv_sem):
    me, coords = coords_of()
    barrier = pltpu.get_barrier_semaphore()
    for d in range(1, n):
        pl.semaphore_signal(barrier, inc=1, device_id=coords((me + d) % n), device_id_type=pl.DeviceIdType.MESH)
    pl.semaphore_wait(barrier, n - 1)
    held[pl.ds(me, 1)] = x_ref[...][None]
    copies = []
    for d in range(1, n):
        c = pltpu.make_async_remote_copy(
            src_ref=x_ref, dst_ref=held.at[me], send_sem=send_sem.at[d], recv_sem=recv_sem.at[d],
            device_id=coords((me + d) % n), device_id_type=pl.DeviceIdType.MESH)
        c.start()
        copies.append(c)
    for c in copies:
        c.wait()
    o_ref[...] = held[...]


def peer_gather(x, n, coords_of, cid):
    return pl.pallas_call(
        functools.partial(peer_kernel, n, coords_of),
        out_shape=jax.ShapeDtypeStruct((n,) + x.shape, x.dtype),
        in_specs=[pl.BlockSpec(memory_space=pltpu.VMEM)],
        out_specs=pl.BlockSpec(memory_space=pltpu.VMEM),
        scratch_shapes=[pltpu.VMEM((n,) + x.shape, x.dtype), pltpu.SemaphoreType.DMA((n,)), pltpu.SemaphoreType.DMA((n,))],
        compiler_params=pltpu.CompilerParams(collective_id=cid, has_side_effects=True),
    )(x)


def along_x():
    here = tuple(lax.axis_index(name) for name in MESH_AXES)
    return here[3], lambda t: here[:3] + (t,)


def along_req():
    here = tuple(lax.axis_index(name) for name in MESH_AXES)
    zs, cs = lax.axis_size("z"), lax.axis_size("c")
    me = (here[0] * zs + here[1]) * cs + here[2]
    return me, lambda t: (t // (zs * cs), (t // cs) % zs, t % cs, here[3])


def stats_kernel(steps, n, w_ref, x_ref, b_ref, v_ref, t_ref, out_ref, m_sc, s_sc, mo_sc, p_sc, mine, held, send_sem, recv_sem):
    j = pl.program_id(1)
    me, coords = along_x()
    barrier = pltpu.get_barrier_semaphore()

    @pl.when(j == 0)
    def _():
        for d in range(1, n):
            pl.semaphore_signal(barrier, inc=1, device_id=coords((me + d) % n), device_id_type=pl.DeviceIdType.MESH)
        m_sc[...] = jnp.full(m_sc.shape, NEG, jnp.float32)
        s_sc[...] = jnp.zeros(s_sc.shape, jnp.float32)
        mo_sc[...] = jnp.zeros(mo_sc.shape, jnp.float32)
        p_sc[...] = jnp.zeros(p_sc.shape, jnp.float32)

    logits = jnp.dot(w_ref[...], x_ref[...], preferred_element_type=jnp.float32)
    logits = logits + b_ref[...]
    tn, tm = logits.shape
    grouped = logits.reshape(tn // SUB, SUB, tm)
    m_old = m_sc[...]
    m_new = jnp.maximum(m_old, jnp.max(jnp.max(grouped, axis=0), axis=0, keepdims=True))
    alpha = jnp.exp(m_old - m_new)
    e = jnp.exp(logits - m_new)
    hit = jnp.where(v_ref[...] == t_ref[...], logits, 0.0)
    s_sc[...] = s_sc[...] * alpha + jnp.sum(e.reshape(tn // SUB, SUB, tm), axis=0)
    mo_sc[...] = mo_sc[...] * alpha + jnp.sum((e * logits).reshape(tn // SUB, SUB, tm), axis=0)
    p_sc[...] = p_sc[...] + jnp.sum(hit.reshape(tn // SUB, SUB, tm), axis=0)
    m_sc[...] = m_new

    @pl.when(j == steps - 1)
    def _():
        mine[0:1, :] = m_sc[...]
        mine[1:2, :] = jnp.sum(s_sc[...], axis=0, keepdims=True)
        mine[2:3, :] = jnp.sum(mo_sc[...], axis=0, keepdims=True)
        mine[3:4, :] = jnp.sum(p_sc[...], axis=0, keepdims=True)
        held[pl.ds(me, 1)] = mine[...][None]
        pl.semaphore_wait(barrier, n - 1)
        copies = []
        for d in range(1, n):
            c = pltpu.make_async_remote_copy(
                src_ref=mine, dst_ref=held.at[me], send_sem=send_sem.at[d], recv_sem=recv_sem.at[d],
                device_id=coords((me + d) % n), device_id_type=pl.DeviceIdType.MESH)
            c.start()
            copies.append(c)
        for c in copies:
            c.wait()
        out_ref[...] = held[...]


def fused_stats(normed_t, piece, bias, vocab_ids, ids, n, tm=1024, tn=1024):
    depth, rows = normed_t.shape
    cols = piece.shape[0]
    grid = (rows // tm, cols // tn)
    assert grid[0] == 1
    return pl.pallas_call(
        functools.partial(stats_kernel, grid[1], n),
        out_shape=jax.ShapeDtypeStruct((n, 4, rows), jnp.float32),
        grid=grid,
        in_specs=[
            pl.BlockSpec((tn, depth), lambda i, j: (j, 0)),
            pl.BlockSpec((depth, tm), lambda i, j: (0, i)),
            pl.BlockSpec((tn, 1), lambda i, j: (j, 0)),
            pl.BlockSpec((tn, 1), lambda i, j: (j, 0)),
            pl.BlockSpec((1, tm), lambda i, j: (0, i)),
        ],
        out_specs=pl.BlockSpec((n, 4, rows), lambda i, j: (0, 0, 0)),
        scratch_shapes=[pltpu.VMEM((1, tm), jnp.float32)] + [pltpu.VMEM((SUB, tm), jnp.float32)] * 3
        + [pltpu.VMEM((4, rows), jnp.float32), pltpu.VMEM((n, 4, rows), jnp.float32),
           pltpu.SemaphoreType.DMA((n,)), pltpu.SemaphoreType.DMA((n,))],
        compiler_params=pltpu.CompilerParams(
            dimension_semantics=("arbitrary", "arbitrary"), collective_id=0, has_side_effects=True
        ),
        cost_estimate=pl.CostEstimate(
            flops=2 * rows * cols * depth,
            transcendentals=rows * cols,
            bytes_accessed=2 * (rows * depth + grid[0] * cols * depth),
        ),
    )(piece, normed_t, bias, vocab_ids, ids)


def chunk_stats(normed, piece, valid, vocab_ids, ids, n):
    bias = jnp.where(valid, 0.0, NEG).astype(jnp.float32)[:, None]
    return fused_stats(normed.T, piece, bias, vocab_ids[:, None], ids[None, :], n)


def merge(stats):
    tops = jnp.stack([s[0] for s in stats])
    top = jnp.max(tops, axis=0)
    factor = jnp.exp(tops - top[None, :])
    total = jnp.sum(factor * jnp.stack([s[1] for s in stats]), axis=0)
    moment = jnp.sum(factor * jnp.stack([s[2] for s in stats]), axis=0)
    pick = jnp.sum(jnp.stack([s[3] for s in stats]), axis=0)
    return top, total, moment, pick


def body(hidden, gain, head, token_ids, lengths, prompt_of):
    rows, part_width = hidden.shape
    splits = lax.axis_size("x")
    column_index = lax.axis_index("x")
    req_count = lax.axis_size(REQ)
    shard_cols = head.shape[1]
    width = part_width * splits

    extra = jnp.zeros((8, part_width), hidden.dtype).at[0].set(gain)
    packed = jnp.concatenate([hidden, extra], axis=0)
    shift = lambda x, d: lax.ppermute(x, "x", [(i, (i + d) % splits) for i in range(splits)])
    from_left = shift(packed, 1)
    from_right = shift(packed, -1)
    from_far = shift(from_left, 1)
    stacked = jnp.stack([packed, from_right, from_far, from_left])
    order = (jnp.arange(splits, dtype=jnp.int32) - column_index) % splits
    stacked = jnp.take(stacked, order, axis=0)
    gathered = jnp.transpose(stacked, (1, 0, 2)).reshape(rows + 8, width)
    widened = gathered[:rows].astype(jnp.float32)
    gain_full = gathered[rows].astype(jnp.float32)
    scale = lax.rsqrt(jnp.sum(widened * widened, axis=1) / width + eps)
    normed = (widened * scale[:, None] * gain_full[None, :]).astype(jnp.bfloat16)

    chunk = 256
    bounds = [(lo, min(lo + chunk, shard_cols)) for lo in range(0, shard_cols, chunk)]
    stats = []
    for lo, hi in bounds:
        part = head[:, lo:hi].T
        if hi - lo < chunk:
            part = jnp.concatenate([part, jnp.zeros((chunk - (hi - lo), part.shape[1]), part.dtype)], axis=0)
        part = with_layout_constraint(part, Layout(major_to_minor=(0, 1)))
        piece = lax.all_gather(part, REQ, axis=0, tiled=False)
        piece = with_layout_constraint(piece, Layout(major_to_minor=(0, 1, 2)))
        piece = piece.reshape(req_count * chunk, piece.shape[2])
        g = jnp.arange(req_count * chunk, dtype=jnp.int32)
        owner = g // chunk
        offset = lo + g % chunk
        valid = offset < hi
        vocab_ids = jnp.where(valid, (owner * splits + column_index) * shard_cols + offset, -1)
        stats.append(chunk_stats(normed, piece, valid, vocab_ids, token_ids, splits))
    everyone = stats[0]

    top, total, moment, picked = merge([tuple(everyone[k, j] for j in range(4)) for k in range(splits)])

    positions = jnp.arange(rows, dtype=jnp.int32)
    live = positions < lengths[0]
    safe_total = jnp.where(live, total, 1.0)
    log_norm = top + jnp.log(safe_total)
    logprob = jnp.where(live, picked - log_norm, 0.0)
    entropy = jnp.where(live, log_norm - moment / safe_total, 0.0)
    onehot = (jnp.arange(PROMPTS, dtype=jnp.int32) == prompt_of[0]).astype(jnp.float32)
    share = rows // splits
    own_logprob = lax.dynamic_slice_in_dim(logprob, column_index * share, share)
    own_entropy = lax.dynamic_slice_in_dim(entropy, column_index * share, share)
    summary = jnp.stack([jnp.sum(entropy), jnp.sum(logprob), lengths[0].astype(jnp.float32)])
    summed = jnp.zeros((8, 128), jnp.float32).at[:PROMPTS, :3].set(onehot[:, None] * summary[None, :])
    summed = jnp.sum(peer_gather(summed, req_count, along_req, 1), axis=0)[:PROMPTS, :3]
    prompt_stats = summed[:, :2] / jnp.maximum(summed[:, 2:3], 1.0)
    return (own_logprob, own_entropy, prompt_stats)


def solution(mesh):
    req_axes = mesh.devices.shape[0] // 8
    fine = Mesh(mesh.devices.reshape(req_axes, 4, 2, mesh.devices.shape[1]), ("y", "z", "c", "x"))
    in_specs = (
        P(REQ, "x"),
        P("x"),
        P(None, REQ + ("x",)),
        P(REQ),
        P(REQ),
        P(REQ),
    )
    out_specs = (P(REQ + ("x",)), P(REQ + ("x",)), P())
    return jax.shard_map(body, mesh=fine, in_specs=in_specs, out_specs=out_specs, check_vma=False)
```

```python
import functools

import jax
import jax.numpy as jnp
from jax import lax
from jax.experimental import pallas as pl
from jax.experimental.pallas import tpu as pltpu
from jax.sharding import Mesh, PartitionSpec as P
from jax.experimental.layout import Layout, with_layout_constraint

PROMPTS = 4
REQ = ("y", "z", "c")
MESH_AXES = ("y", "z", "c", "x")
NEG = -1e30
SUB = 8

eps = 1e-06


def along_x():
    here = tuple(lax.axis_index(name) for name in MESH_AXES)
    return here[3], lambda t: here[:3] + (t,)


def along_req():
    here = tuple(lax.axis_index(name) for name in MESH_AXES)
    zs, cs = lax.axis_size("z"), lax.axis_size("c")
    me = (here[0] * zs + here[1]) * cs + here[2]
    return me, lambda t: (t // (zs * cs), (t // cs) % zs, t % cs, here[3])


def stats_kernel(steps, n, nr, w_ref, x_ref, b_ref, v_ref, t_ref, len_ref, pr_ref, lp_ref, en_ref, ps_ref, m_sc, s_sc, mo_sc, p_sc, mine, held, send_sem, recv_sem, tile, held2, send2, recv2):
    j = pl.program_id(1)
    me, coords = along_x()
    mr, coords_r = along_req()
    barrier = pltpu.get_barrier_semaphore()

    @pl.when(j == 0)
    def _():
        for d in range(1, n):
            pl.semaphore_signal(barrier, inc=1, device_id=coords((me + d) % n), device_id_type=pl.DeviceIdType.MESH)
        for d in range(1, nr):
            pl.semaphore_signal(barrier, inc=1, device_id=coords_r((mr + d) % nr), device_id_type=pl.DeviceIdType.MESH)
        m_sc[...] = jnp.full(m_sc.shape, NEG, jnp.float32)
        s_sc[...] = jnp.zeros(s_sc.shape, jnp.float32)
        mo_sc[...] = jnp.zeros(mo_sc.shape, jnp.float32)
        p_sc[...] = jnp.zeros(p_sc.shape, jnp.float32)

    logits = jnp.dot(w_ref[...], x_ref[...], preferred_element_type=jnp.float32)
    logits = logits + jnp.where(v_ref[...] < 0, NEG, 0.0)
    tn, tm = logits.shape
    grouped = logits.reshape(tn // SUB, SUB, tm)
    m_old = m_sc[...]
    m_new = jnp.maximum(m_old, jnp.max(jnp.max(grouped, axis=0), axis=0, keepdims=True))
    alpha = jnp.exp(m_old - m_new)
    e = jnp.exp(logits - m_new)
    hit = jnp.where(v_ref[...] == t_ref[...], logits, 0.0)
    s_sc[...] = s_sc[...] * alpha + jnp.sum(e.reshape(tn // SUB, SUB, tm), axis=0)
    mo_sc[...] = mo_sc[...] * alpha + jnp.sum((e * logits).reshape(tn // SUB, SUB, tm), axis=0)
    p_sc[...] = p_sc[...] + jnp.sum(hit.reshape(tn // SUB, SUB, tm), axis=0)
    m_sc[...] = m_new

    @pl.when(j == steps - 1)
    def _():
        mine[0:1, :] = m_sc[...]
        mine[1:2, :] = jnp.sum(s_sc[...], axis=0, keepdims=True)
        mine[2:3, :] = jnp.sum(mo_sc[...], axis=0, keepdims=True)
        mine[3:4, :] = jnp.sum(p_sc[...], axis=0, keepdims=True)
        held[pl.ds(me, 1)] = mine[...][None]
        pl.semaphore_wait(barrier, n - 1 + nr - 1)
        copies = []
        for d in range(1, n):
            c = pltpu.make_async_remote_copy(
                src_ref=mine, dst_ref=held.at[me], send_sem=send_sem.at[d], recv_sem=recv_sem.at[d],
                device_id=coords((me + d) % n), device_id_type=pl.DeviceIdType.MESH)
            c.start()
            copies.append(c)
        for c in copies:
            c.wait()
        everyone = held[...]
        tops = everyone[:, 0, :]
        top = jnp.max(tops, axis=0, keepdims=True)
        factor = jnp.exp(tops - top)
        total = jnp.sum(factor * everyone[:, 1, :], axis=0, keepdims=True)
        moment = jnp.sum(factor * everyone[:, 2, :], axis=0, keepdims=True)
        picked = jnp.sum(everyone[:, 3, :], axis=0, keepdims=True)
        length = len_ref[0]
        live = lax.broadcasted_iota(jnp.int32, top.shape, 1) < length
        safe_total = jnp.where(live, total, 1.0)
        log_norm = top + jnp.log(safe_total)
        logprob = jnp.where(live, picked - log_norm, 0.0)
        entropy = jnp.where(live, log_norm - moment / safe_total, 0.0)
        lp_ref[...] = logprob
        en_ref[...] = entropy
        row = lax.broadcasted_iota(jnp.int32, tile.shape, 0)
        col = lax.broadcasted_iota(jnp.int32, tile.shape, 1)
        sums = jnp.where(col == 0, jnp.sum(entropy), jnp.where(col == 1, jnp.sum(logprob), length.astype(jnp.float32)))
        tile[...] = jnp.where((row == pr_ref[0]) & (col < 3), sums, 0.0)
        held2[pl.ds(mr, 1)] = tile[...][None]
        copies = []
        for d in range(1, nr):
            c = pltpu.make_async_remote_copy(
                src_ref=tile, dst_ref=held2.at[mr], send_sem=send2.at[d], recv_sem=recv2.at[d],
                device_id=coords_r((mr + d) % nr), device_id_type=pl.DeviceIdType.MESH)
            c.start()
            copies.append(c)
        for c in copies:
            c.wait()
        ps_ref[...] = jnp.sum(held2[...], axis=0)


def fused_stats(normed_t, piece, bias, vocab_ids, ids, lengths, prompt_of, n, nr, tm=1024, tn=1024):
    depth, rows = normed_t.shape
    cols = piece.shape[0]
    grid = (rows // tm, cols // tn)
    assert grid[0] == 1
    return pl.pallas_call(
        functools.partial(stats_kernel, grid[1], n, nr),
        out_shape=(jax.ShapeDtypeStruct((1, rows), jnp.float32), jax.ShapeDtypeStruct((1, rows), jnp.float32),
                   jax.ShapeDtypeStruct((8, 128), jnp.float32)),
        grid=grid,
        in_specs=[
            pl.BlockSpec((tn, depth), lambda i, j: (j, 0)),
            pl.BlockSpec((depth, tm), lambda i, j: (0, i)),
            pl.BlockSpec((tn, 1), lambda i, j: (j, 0)),
            pl.BlockSpec((tn, 1), lambda i, j: (j, 0)),
            pl.BlockSpec((1, tm), lambda i, j: (0, i)),
            pl.BlockSpec(memory_space=pltpu.SMEM),
            pl.BlockSpec(memory_space=pltpu.SMEM),
        ],
        out_specs=(pl.BlockSpec((1, rows), lambda i, j: (0, 0)), pl.BlockSpec((1, rows), lambda i, j: (0, 0)),
                   pl.BlockSpec((8, 128), lambda i, j: (0, 0))),
        scratch_shapes=[pltpu.VMEM((1, tm), jnp.float32)] + [pltpu.VMEM((SUB, tm), jnp.float32)] * 3
        + [pltpu.VMEM((4, rows), jnp.float32), pltpu.VMEM((n, 4, rows), jnp.float32),
           pltpu.SemaphoreType.DMA((n,)), pltpu.SemaphoreType.DMA((n,)),
           pltpu.VMEM((8, 128), jnp.float32), pltpu.VMEM((nr, 8, 128), jnp.float32),
           pltpu.SemaphoreType.DMA((nr,)), pltpu.SemaphoreType.DMA((nr,))],
        compiler_params=pltpu.CompilerParams(
            dimension_semantics=("arbitrary", "arbitrary"), collective_id=0, has_side_effects=True
        ),
        cost_estimate=pl.CostEstimate(
            flops=2 * rows * cols * depth,
            transcendentals=rows * cols,
            bytes_accessed=2 * (rows * depth + grid[0] * cols * depth),
        ),
    )(piece, normed_t, bias, vocab_ids, ids, lengths, prompt_of)


def chunk_stats(normed, piece, valid, vocab_ids, ids, lengths, prompt_of, n, nr):
    bias = jnp.where(valid, 0.0, NEG).astype(jnp.float32)[:, None]
    return fused_stats(normed.T, piece, bias, vocab_ids[:, None], ids[None, :], lengths, prompt_of, n, nr)


def body(hidden, gain, head, token_ids, lengths, prompt_of):
    rows, part_width = hidden.shape
    splits = lax.axis_size("x")
    column_index = lax.axis_index("x")
    req_count = lax.axis_size(REQ)
    shard_cols = head.shape[1]
    width = part_width * splits

    extra = jnp.zeros((8, part_width), hidden.dtype).at[0].set(gain)
    packed = jnp.concatenate([hidden, extra], axis=0)
    shift = lambda x, d: lax.ppermute(x, "x", [(i, (i + d) % splits) for i in range(splits)])
    from_left = shift(packed, 1)
    from_right = shift(packed, -1)
    from_far = shift(from_left, 1)
    stacked = jnp.stack([packed, from_right, from_far, from_left])
    order = (jnp.arange(splits, dtype=jnp.int32) - column_index) % splits
    stacked = jnp.take(stacked, order, axis=0)
    gathered = jnp.transpose(stacked, (1, 0, 2)).reshape(rows + 8, width)
    widened = gathered[:rows].astype(jnp.float32)
    gain_full = gathered[rows].astype(jnp.float32)
    scale = lax.rsqrt(jnp.sum(widened * widened, axis=1) / width + eps)
    normed = (widened * scale[:, None] * gain_full[None, :]).astype(jnp.bfloat16)

    chunk = 256
    bounds = [(lo, min(lo + chunk, shard_cols)) for lo in range(0, shard_cols, chunk)]
    stats = []
    for lo, hi in bounds:
        part = head[:, lo:hi].T
        if hi - lo < chunk:
            part = jnp.concatenate([part, jnp.zeros((chunk - (hi - lo), part.shape[1]), part.dtype)], axis=0)
        part = with_layout_constraint(part, Layout(major_to_minor=(0, 1)))
        piece = lax.all_gather(part, REQ, axis=0, tiled=False)
        piece = with_layout_constraint(piece, Layout(major_to_minor=(0, 1, 2)))
        piece = piece.reshape(req_count * chunk, piece.shape[2])
        g = jnp.arange(req_count * chunk, dtype=jnp.int32)
        owner = g // chunk
        offset = lo + g % chunk
        valid = offset < hi
        vocab_ids = jnp.where(valid, (owner * splits + column_index) * shard_cols + offset, -1)
        stats.append(chunk_stats(normed, piece, valid, vocab_ids, token_ids, lengths, prompt_of, splits, req_count))
    logprob, entropy, summed = stats[0]
    logprob = logprob[0]
    entropy = entropy[0]
    share = rows // splits
    own_logprob = lax.dynamic_slice_in_dim(logprob, column_index * share, share)
    own_entropy = lax.dynamic_slice_in_dim(entropy, column_index * share, share)
    summed = summed[:PROMPTS, :3]
    prompt_stats = summed[:, :2] / jnp.maximum(summed[:, 2:3], 1.0)
    return (own_logprob, own_entropy, prompt_stats)


def solution(mesh):
    req_axes = mesh.devices.shape[0] // 8
    fine = Mesh(mesh.devices.reshape(req_axes, 4, 2, mesh.devices.shape[1]), ("y", "z", "c", "x"))
    in_specs = (
        P(REQ, "x"),
        P("x"),
        P(None, REQ + ("x",)),
        P(REQ),
        P(REQ),
        P(REQ),
    )
    out_specs = (P(REQ + ("x",)), P(REQ + ("x",)), P())
    return jax.shard_map(body, mesh=fine, in_specs=in_specs, out_specs=out_specs, check_vma=False)
```
